32 devices in a mesh: span: 8 (over y, x, core), head: 4 (over z).
Axes of the slice: x: 2, y: 2, z: 4, core: 2. Of those that a mesh axis runs over, the one named last changes fastest.
Arguments:
- neighbour_query: bfloat16 [8192, 4096], P('span', 'head'), may hold values from -12 to 12
- neighbour_key: bfloat16 [8192, 4096], P('span', 'head'), may hold values from -6 to 6
- neighbour_value: bfloat16 [8192, 4096], P('span', 'head'), may hold values from -12.2 to 12.2
- segment_key: bfloat16 [2048, 4096], P('span', 'head'), may hold values from -30 to 30
- segment_value: bfloat16 [2048, 4096], P('span', 'head'), may hold values from -6 to 6
- decoder_query: bfloat16 [2048, 4096], P('span', 'head'), may hold values from -24 to 24
- sources: int32 [32, 2], P('span'), may hold values from 0 to 31, as said below
Outputs:
- blended: bfloat16 [2048, 4096], P('span', 'head')
The draws below stay inside these ranges and needn't reach their ends.
Inputs may be any that keep to these rules, and one draw needn't show every extreme that they name: `sources`: the segments of index o of span are o * 4 to (o + 1) * 4 - 1. Among the 8 entries of the segments of one index of span, at most 2 name segments of one index of span, and in every such block some index is named exactly 2 times.
All inputs are finite; a program needn't handle non-finite values.
Results may differ from the reference program's by a relative error of at most 0.035.
Values may be sent and summed in bfloat16 or wider, within the bound.
A program may use at most 192 MiB of HBM per device.

```python
import math
import jax
import jax.numpy as jnp
from jax import lax

HEAD_DIM = 128
SEG_LEN = 64
NBR_LEN = 128
NEIGHBOURS = 2
SEG_DEV = 4
HIDDEN_COLS = 4096
SEGMENTS = 32
CAPACITY = 2
N_SPAN = 8


def rising_scales():
    return 0.3 * jnp.exp(math.log(10.0) * jnp.arange(HIDDEN_COLS, dtype=jnp.float32) / HIDDEN_COLS)


def draw_sources(key, part):
    keys = jax.random.split(jax.random.fold_in(key, 26), 5)
    per_block = SEG_DEV * NEIGHBOURS
    slot_count_total = N_SPAN * CAPACITY
    favoured_rows = jax.random.randint(keys[0], (N_SPAN,), 0, 4)
    slot_holder_index = jnp.arange(slot_count_total) // CAPACITY
    random_jitter = jax.random.randint(keys[1], (N_SPAN, slot_count_total), 0, 1024)
    hotspot_row = jax.random.randint(keys[2], (N_SPAN,), 0, N_SPAN)
    extra_score = jnp.where(slot_holder_index[None, :] == hotspot_row[:, None], 8, 0)
    logit_scores = ((favoured_rows[slot_holder_index][None, :] + extra_score) * 1024 + random_jitter) * slot_count_total + jnp.arange(slot_count_total)[None, :]
    top_values, top_index = lax.top_k(logit_scores, per_block)
    owners = slot_holder_index[top_index]
    mixing = jax.random.randint(keys[3], (N_SPAN, per_block), 0, 1 << 20) * per_block + jnp.arange(per_block)[None, :]
    shuffle = jnp.argsort(mixing, axis=1)
    owners = jnp.take_along_axis(owners, shuffle, axis=1)
    within = jax.random.randint(keys[4], (N_SPAN, per_block), 0, SEG_DEV)
    return (owners * SEG_DEV + within).reshape(SEGMENTS, NEIGHBOURS).astype(jnp.int32)


def draw_neighbour_query(key, part):
    row_total = SEGMENTS * NEIGHBOURS * NBR_LEN
    sample_key = jax.random.fold_in(key, 21)
    return jnp.clip(2.0 * jax.random.normal(sample_key, (row_total, HIDDEN_COLS), jnp.float32), -12.0, 12.0).astype(jnp.bfloat16)


def draw_neighbour_key(key, part):
    row_total = SEGMENTS * NEIGHBOURS * NBR_LEN
    sample_key = jax.random.fold_in(key, 22)
    return jnp.clip(jax.random.normal(sample_key, (row_total, HIDDEN_COLS), jnp.float32), -6.0, 6.0).astype(jnp.bfloat16)


def draw_neighbour_value(key, part):
    row_total = SEGMENTS * NEIGHBOURS * NBR_LEN
    sample_key = jax.random.fold_in(key, 23)
    filler = jnp.clip(jax.random.normal(sample_key, (row_total, HIDDEN_COLS), jnp.float32), -4.0, 4.0)
    return (filler * rising_scales()[None, :]).astype(jnp.bfloat16)


def draw_segment_key(key, part):
    row_total = SEGMENTS * SEG_LEN
    sample_key = jax.random.fold_in(key, 24)
    return jnp.clip(2.0 * jax.random.normal(sample_key, (row_total, HIDDEN_COLS), jnp.float32), -12.0, 12.0).astype(jnp.bfloat16)


def draw_decoder_query(key, part):
    row_total = SEGMENTS * SEG_LEN
    sample_key = jax.random.fold_in(key, 25)
    return jnp.clip(3.0 * jax.random.normal(sample_key, (row_total, HIDDEN_COLS), jnp.float32), -18.0, 18.0).astype(jnp.bfloat16)


def block_levels(rng, extent, pieces, low, high):
    loudness = 1.0
    for dim, shards_of in pieces:
        draws = jax.random.uniform(jax.random.fold_in(jax.random.fold_in(rng, 6), dim), (shards_of,), jnp.float32, low / len(pieces), high / len(pieces))
        loudness = loudness * jnp.repeat(jnp.exp(draws), extent[dim] // shards_of).reshape((-1,) + (1,) * (len(extent) - 1 - dim))
    return loudness


def normal_values(key, extent, spread, most, cuts=(), held_as=jnp.bfloat16):
    values = jax.random.normal(key, extent, jnp.float32) * spread
    if len(cuts) > 0:
        values = block_levels(key, extent, cuts, -0.22, 0.18) * values
    return jnp.clip(values, min=-most, max=most).astype(held_as)


def setup_inputs(seed: int = 0) -> dict:
    seeds = jax.random.split(jax.random.key(seed), 8)
    neighbour_query = draw_neighbour_query(jax.random.fold_in(seeds[7], 71), 0)
    neighbour_key = draw_neighbour_key(jax.random.fold_in(seeds[7], 71), 0)
    neighbour_value = draw_neighbour_value(jax.random.fold_in(seeds[7], 71), 0)
    segment_key = draw_segment_key(jax.random.fold_in(seeds[7], 71), 0)
    segment_value = normal_values(seeds[4], (SEGMENTS * SEG_LEN, HIDDEN_COLS), 1.0, 6.0, ((0, 8), (1, 4)))
    decoder_query = draw_decoder_query(jax.random.fold_in(seeds[7], 71), 0)
    sources = draw_sources(jax.random.fold_in(seeds[7], 71), 0)
    return {"neighbour_query": neighbour_query, "neighbour_key": neighbour_key, "neighbour_value": neighbour_value, "segment_key": segment_key, "segment_value": segment_value, "decoder_query": decoder_query, "sources": sources}


epsilon = 1e-06

def attend(query_rows, key_rows, value_rows):
    groups, length, columns = query_rows.shape
    head_count = columns // HEAD_DIM
    query_heads = query_rows.astype(jnp.float32).reshape(groups, length, head_count, HEAD_DIM)
    key_heads = key_rows.astype(jnp.float32).reshape(groups, key_rows.shape[1], head_count, HEAD_DIM)
    value_heads = value_rows.astype(jnp.float32).reshape(groups, value_rows.shape[1], head_count, HEAD_DIM)
    logit_scores = jnp.einsum('bqhd,bkhd->bhqk', query_heads, key_heads) * HEAD_DIM ** (-0.5)
    logit_scores = logit_scores - lax.optimization_barrier(jnp.max(logit_scores, axis=-1, keepdims=True))
    weights = jnp.exp(logit_scores)
    weights = (weights / lax.optimization_barrier(jnp.sum(weights, axis=-1, keepdims=True))).astype(jnp.bfloat16)
    output = jnp.einsum('bhqk,bkhd->bqhd', weights.astype(jnp.float32), value_heads)
    return output.reshape(groups, length, columns)

def normalize(rows):
    wide = rows.astype(jnp.float32)
    meansq = lax.optimization_barrier(jnp.mean(wide * wide, axis=-1, keepdims=True))
    return (wide * lax.rsqrt(meansq + epsilon)).astype(jnp.bfloat16)

def reference(neighbour_query, neighbour_key, neighbour_value, segment_key, segment_value, decoder_query, sources):
    columns = neighbour_query.shape[1]
    per_device = SEG_DEV * NEIGHBOURS
    all_keys = segment_key.reshape(SEGMENTS, SEG_LEN, columns)
    all_values = segment_value.reshape(SEGMENTS, SEG_LEN, columns)

    def encode(group):
        query_rows, key_rows, value_rows, listed = group
        self_out = attend(query_rows, key_rows, value_rows).astype(jnp.bfloat16)
        cross_query = normalize(self_out)
        crossed = attend(cross_query, all_keys[listed], all_values[listed]).astype(jnp.bfloat16)
        return (self_out.astype(jnp.float32) + crossed.astype(jnp.float32)).astype(jnp.bfloat16)

    def shaped(array):
        return array.reshape(N_SPAN, per_device, NBR_LEN, columns)
    listed_all = sources.reshape(N_SPAN, per_device).astype(jnp.int32)
    encoded = lax.map(encode, (shaped(neighbour_query), shaped(neighbour_key), shaped(neighbour_value), listed_all))
    encoded = encoded.reshape(SEGMENTS, NEIGHBOURS * NBR_LEN, columns)
    prior = jnp.concatenate([jnp.zeros((1, NEIGHBOURS * NBR_LEN, columns), jnp.bfloat16), encoded[:-1]], axis=0)

    def decode(group):
        query_rows, value_rows = group
        return attend(query_rows, normalize(value_rows), value_rows).astype(jnp.bfloat16)
    blended = lax.map(decode, (decoder_query.reshape(N_SPAN, SEG_DEV, SEG_LEN, columns), prior.reshape(N_SPAN, SEG_DEV, NEIGHBOURS * NBR_LEN, columns)))
    return blended.reshape(SEGMENTS * SEG_LEN, columns)
```

```python
import functools

import jax
import jax.numpy as jnp
from jax import lax
from jax.experimental import pallas as pl
from jax.experimental.pallas import tpu as pltpu
from jax.sharding import PartitionSpec as P

HEAD_DIM = 128
SEG_LEN = 64
NBR_LEN = 128
NEIGHBOURS = 2
SEG_DEV = 4


epsilon = 1e-06


def from_behind(x, axis, by):
    count = lax.axis_size(axis)
    pairs = [(i, i + by) for i in range(count) if 0 <= i + by < count]
    return lax.ppermute(x, axis, pairs)


def attend(query_rows, key_rows, value_rows):
    groups, length, columns = query_rows.shape
    head_count = columns // HEAD_DIM
    query_heads = query_rows.reshape(groups, length, head_count, HEAD_DIM)
    key_heads = key_rows.reshape(groups, key_rows.shape[1], head_count, HEAD_DIM)
    value_heads = value_rows.reshape(groups, value_rows.shape[1], head_count, HEAD_DIM)
    logit_scores = jnp.einsum(
        "bqhd,bkhd->bhqk", query_heads, key_heads, preferred_element_type=jnp.float32
    ) * HEAD_DIM ** (-0.5)
    logit_scores = logit_scores - jnp.max(logit_scores, axis=-1, keepdims=True)
    weights = jnp.exp(logit_scores)
    weights = (weights / jnp.sum(weights, axis=-1, keepdims=True)).astype(jnp.bfloat16)
    output = jnp.einsum("bhqk,bkhd->bqhd", weights, value_heads, preferred_element_type=jnp.float32)
    return output.reshape(groups, length, columns)


def squares(rows):
    wide = rows.astype(jnp.float32)
    return jnp.sum(wide * wide, axis=-1)


def normalize(rows, totals, full_width):
    scale = lax.rsqrt(totals / full_width + epsilon)
    return (rows.astype(jnp.float32) * scale[:, None]).astype(jnp.bfloat16)


def body(
    neighbour_query,
    neighbour_key,
    neighbour_value,
    segment_key,
    segment_value,
    decoder_query,
    sources,
):
    columns = neighbour_query.shape[1]
    full_width = columns * lax.axis_size("head")
    devices = lax.axis_size("span")
    per_device = SEG_DEV * NEIGHBOURS
    capacity = max(2, 2 * per_device // devices)
    panel_rows = NEIGHBOURS * NBR_LEN
    self_out = attend(
        neighbour_query.reshape(per_device, NBR_LEN, columns),
        neighbour_key.reshape(per_device, NBR_LEN, columns),
        neighbour_value.reshape(per_device, NBR_LEN, columns),
    ).astype(jnp.bfloat16)
    flat_self = self_out.reshape(per_device * NBR_LEN, columns)
    totals = lax.psum(squares(flat_self), "head")
    cross_query = normalize(flat_self, totals, full_width).reshape(per_device, NBR_LEN, columns)
    listed = sources.reshape(per_device)
    owners = listed // SEG_DEV
    within = listed % SEG_DEV
    position = jnp.arange(per_device)
    earlier = (owners[:, None] == owners[None, :]) & (position[:, None] > position[None, :])
    ranked = jnp.sum(earlier.astype(jnp.int32), axis=1)
    slots = owners * capacity + ranked
    picked = (slots[:, None] == jnp.arange(devices * capacity)[None, :]).astype(jnp.int32)
    request = jnp.sum(picked * (within + 1)[:, None], axis=0).reshape(devices, capacity)
    asked = lax.all_to_all(request, "span", split_axis=0, concat_axis=0, tiled=True)
    wanted = jnp.maximum(asked - 1, 0).reshape(devices * capacity)
    own_keys = segment_key.reshape(SEG_DEV, SEG_LEN, columns)[wanted]
    own_values = segment_value.reshape(SEG_DEV, SEG_LEN, columns)[wanted]
    got_keys, got_values = (
        lax.all_to_all(
            own_keys.reshape(devices, capacity, SEG_LEN, columns),
            "span",
            split_axis=0,
            concat_axis=0,
            tiled=True,
        ),
        lax.all_to_all(
            own_values.reshape(devices, capacity, SEG_LEN, columns),
            "span",
            split_axis=0,
            concat_axis=0,
            tiled=True,
        ),
    )
    source_keys = got_keys.reshape(devices * capacity, SEG_LEN, columns)[slots]
    source_values = got_values.reshape(devices * capacity, SEG_LEN, columns)[slots]
    crossed = attend(cross_query, source_keys, source_values).astype(jnp.bfloat16)
    encoded = (self_out.astype(jnp.float32) + crossed.astype(jnp.float32)).astype(jnp.bfloat16)
    encoded = encoded.reshape(per_device * NBR_LEN, columns)
    key_totals = lax.psum(squares(encoded), "head")
    keys_all = normalize(encoded, key_totals, full_width)
    before_keys, before_values = from_behind(
        (keys_all[-panel_rows:], encoded[-panel_rows:]), "span", 1
    )
    used_keys = jnp.concatenate([before_keys, keys_all[:-panel_rows]], axis=0)
    used_values = jnp.concatenate([before_values, encoded[:-panel_rows]], axis=0)
    blended = attend(
        decoder_query.reshape(SEG_DEV, SEG_LEN, columns),
        used_keys.reshape(SEG_DEV, panel_rows, columns),
        used_values.reshape(SEG_DEV, panel_rows, columns),
    ).astype(jnp.bfloat16)
    return blended.reshape(SEG_DEV * SEG_LEN, columns)


MESH = pl.DeviceIdType.MESH
GROUPS = 4


def dot_t(a, b):
    return lax.dot_general(a, b, (((1,), (1,)), ((), ())), preferred_element_type=jnp.float32)


def dot(a, b):
    return lax.dot_general(a, b, (((1,), (0,)), ((), ())), preferred_element_type=jnp.float32)


def kernel(
    heads_axis, full_width,
    src_ref, nq_hbm, nk_hbm, nv_hbm, sk_hbm, sv_hbm, dq_hbm, out_ref,
    nq, nk, nv, dq, *rest,
):
    kbufs, vbufs = rest[:GROUPS], rest[GROUPS:2 * GROUPS]
    (own_out, enc, squares_acc, row_scale, key_scale,
     stat1, stat2, peer1, peer2, behind2,
     in_sem, dq_sem, local_sem, send_sem, recv_sem,
     stat_send, stat_recv, prior_send, prior_recv) = rest[2 * GROUPS:]
    per_device = nq.shape[0]
    seg_dev = dq.shape[0]
    columns = nq.shape[2]
    width = columns // GROUPS
    group_heads = width // HEAD_DIM
    span = lax.axis_size("span")
    me = lax.axis_index("span")
    lane = lax.axis_index("head")
    core, across, along = me ^ 1, me ^ 2, me ^ 4
    after = lax.rem(me + 1, span)
    before = lax.rem(me + span - 1, span)
    softmax_scale = HEAD_DIM ** (-0.5)

    for i in range(per_device):
        for a, (hbm, vm) in enumerate(((nq_hbm, nq), (nk_hbm, nk), (nv_hbm, nv))):
            pltpu.make_async_copy(hbm.at[i], vm.at[i], in_sem.at[a, i]).start()
    dq_copy = pltpu.make_async_copy(dq_hbm, dq, dq_sem)
    dq_copy.start()

    barrier = pltpu.get_barrier_semaphore()
    greeted = 0
    for target in (core, across, along):
        pl.semaphore_signal(barrier, inc=1, device_id={"span": target, "head": lane}, device_id_type=MESH)
        greeted += 1
    for k in range(1, heads_axis):
        other = lax.rem(lane + k, heads_axis)
        pl.semaphore_signal(barrier, inc=1, device_id={"span": me, "head": other}, device_id_type=MESH)
        greeted += 1
    for k in range(heads_axis):
        other = lax.rem(lane + k, heads_axis)
        for target in (after, before):
            pl.semaphore_signal(barrier, inc=1, device_id={"span": target, "head": other}, device_id_type=MESH)
            greeted += 1
    pl.semaphore_wait(barrier, greeted)

    chunks = 2 * GROUPS

    def buffer(j):
        return (kbufs, vbufs)[j % 2][j // 2]

    def source(j):
        hbm = (sk_hbm, sv_hbm)[j % 2]
        return hbm.at[:, :, pl.ds((j // 2) * width, width)]

    def block(j, owner):
        return buffer(j).at[pl.ds(owner * seg_dev, seg_dev)]

    def half(j, owner, part):
        rows = seg_dev // 2
        return buffer(j).at[pl.ds(owner * seg_dev + part * rows, rows)]

    sent = {}

    def push(kind, j, src, dst, target):
        copy = pltpu.make_async_remote_copy(
            src_ref=src, dst_ref=dst, send_sem=send_sem.at[kind, j], recv_sem=recv_sem.at[kind, j],
            device_id={"span": target, "head": lane}, device_id_type=MESH)
        copy.start()
        sent[kind, j] = copy

    def direct(j):
        push(0, j, source(j), block(j, me), across)
        push(1, j, source(j), block(j, me), along)

    local = []
    direct(0)
    direct(1)
    for j in range(chunks):
        push(4, j, source(j), block(j, me), core)
        copy = pltpu.make_async_copy(source(j), block(j, me), local_sem.at[j])
        copy.start()
        local.append(copy)

    def forward(j):
        sent[2, j].wait_recv()
        sent[3, j].wait_recv()
        push(7, j, block(j, me ^ 6), block(j, me ^ 6), core)

    def step(j):
        sent[1, j].wait_recv()
        push(2, j, half(j, along, 0), half(j, along, 0), across)
        sent[0, j].wait_recv()
        push(3, j, half(j, across, 1), half(j, across, 1), along)
        if j + 2 < chunks:
            direct(j + 2)
        push(5, j, block(j, across), block(j, across), core)
        push(6, j, block(j, along), block(j, along), core)
        if j >= 1:
            forward(j - 1)

    def arrived(j):
        local[j].wait()
        for kind in (4, 5, 6, 7):
            sent[kind, j].wait_recv()

    ones = jnp.ones((NBR_LEN, HEAD_DIM), jnp.bfloat16)

    def self_step(i, carry):
        for a, (hbm, vm) in enumerate(((nq_hbm, nq), (nk_hbm, nk), (nv_hbm, nv))):
            pltpu.make_async_copy(hbm.at[i], vm.at[i], in_sem.at[a, i]).wait()
        total = jnp.zeros((NBR_LEN, HEAD_DIM), jnp.float32)
        for h in range(columns // HEAD_DIM):
            cols = pl.ds(h * HEAD_DIM, HEAD_DIM)
            scores = dot_t(nq[i, :, cols], nk[i, :, cols]) * softmax_scale
            weights = jnp.exp(scores - jnp.max(scores, axis=-1, keepdims=True)).astype(jnp.bfloat16)
            o = (dot(weights, nv[i, :, cols]) / dot(weights, ones)).astype(jnp.bfloat16)
            own_out[h // group_heads, i, :, pl.ds((h % group_heads) * HEAD_DIM, HEAD_DIM)] = o
            wide = o.astype(jnp.float32)
            total = total + wide * wide
        stat1[pl.ds(i, 1), :] = jnp.sum(total.T, axis=0, keepdims=True)
        return carry

    def exchange(kind, stat, peer):
        out = []
        for k in range(1, heads_axis):
            other = lax.rem(lane + k, heads_axis)
            copy = pltpu.make_async_remote_copy(
                src_ref=stat, dst_ref=peer.at[k - 1],
                send_sem=stat_send.at[kind, k - 1], recv_sem=stat_recv.at[kind, k - 1],
                device_id={"span": me, "head": other}, device_id_type=MESH)
            copy.start()
            out.append(copy)
        return out

    def cross_step(g, i):
        kb, vb = kbufs[g], vbufs[g]
        segment = src_ref[i]
        scale = row_scale[i, :, :SEG_LEN]
        key_rows = kb[segment]
        value_rows = vb[segment]
        total = jnp.zeros((NBR_LEN, HEAD_DIM), jnp.float32)
        for h in range(group_heads):
            lo, hi = h * HEAD_DIM, (h + 1) * HEAD_DIM
            first = own_out[g, i, :, pl.ds(lo, HEAD_DIM)]
            scores = dot_t(first, key_rows[:, lo:hi]) * scale
            weights = jnp.exp(scores - jnp.max(scores, axis=-1, keepdims=True)).astype(jnp.bfloat16)
            crossed = (dot(weights, value_rows[:, lo:hi]) / dot(weights, ones[:SEG_LEN])).astype(jnp.bfloat16)
            both = (first.astype(jnp.float32) + crossed.astype(jnp.float32)).astype(jnp.bfloat16)
            enc[g, NEIGHBOURS + i, :, pl.ds(lo, HEAD_DIM)] = both
            wide = both.astype(jnp.float32)
            total = total + wide * wide
        if g > 0:
            total = total + squares_acc[i]
        if g < GROUPS - 1:
            squares_acc[i] = total
        else:
            stat2[pl.ds(i, 1), :] = jnp.sum(total.T, axis=0, keepdims=True)

    prior = []

    def cross(g):
        arrived(2 * g)
        arrived(2 * g + 1)
        for i in range(per_device - NEIGHBOURS, per_device):
            cross_step(g, i)
        copy = pltpu.make_async_remote_copy(
            src_ref=enc.at[g, pl.ds(per_device, NEIGHBOURS)], dst_ref=enc.at[g, pl.ds(0, NEIGHBOURS)],
            send_sem=prior_send.at[g], recv_sem=prior_recv.at[g],
            device_id={"span": after, "head": lane}, device_id_type=MESH)
        copy.start()
        prior.append(copy)

        def rest_step(t, carry):
            for b in range(2):
                cross_step(g, 2 * t + b)
            return carry

        lax.fori_loop(0, (per_device - NEIGHBOURS) // 2, rest_step, 0)

    quarter = per_device // 4
    for j in range(4):
        lax.fori_loop(j * quarter, (j + 1) * quarter, self_step, 0)
        step(j)
    first_stats = exchange(0, stat1, peer1)
    step(4)
    for copy in first_stats:
        copy.wait_recv()
    total1 = stat1[...]
    for k in range(heads_axis - 1):
        total1 = total1 + peer1[k]
    total1 = lax.rsqrt(total1 / full_width + epsilon) * softmax_scale
    for i in range(per_device):
        row_scale[i] = jnp.broadcast_to(total1[i:i + 1], (NBR_LEN, NBR_LEN)).T
    cross(0)
    step(5)
    step(6)
    cross(1)
    step(7)
    cross(2)
    forward(7)
    cross(3)

    second_stats = exchange(1, stat2, peer2)
    behind_stats = []
    for k in range(heads_axis):
        other = lax.rem(lane + k, heads_axis)
        copy = pltpu.make_async_remote_copy(
            src_ref=stat2, dst_ref=behind2.at[k],
            send_sem=stat_send.at[2, k], recv_sem=stat_recv.at[2, k],
            device_id={"span": after, "head": other}, device_id_type=MESH)
        copy.start()
        behind_stats.append(copy)
    dq_copy.wait()
    for copy in second_stats:
        copy.wait_recv()
    total2 = stat2[...]
    for k in range(heads_axis - 1):
        total2 = total2 + peer2[k]
    key_scale[pl.ds(NEIGHBOURS, per_device), :] = lax.rsqrt(total2 / full_width + epsilon) * softmax_scale

    def decode_step(u, carry):
        scales = [key_scale[pl.ds(NEIGHBOURS * u + n, 1), :] for n in range(NEIGHBOURS)]
        scale = jnp.concatenate(scales, axis=1)
        for h in range(columns // HEAD_DIM):
            g, cols = h // group_heads, pl.ds((h % group_heads) * HEAD_DIM, HEAD_DIM)
            rows = enc[g, pl.ds(NEIGHBOURS * u, NEIGHBOURS), :, cols].reshape(NEIGHBOURS * NBR_LEN, HEAD_DIM)
            scores = dot_t(dq[u, :, pl.ds(h * HEAD_DIM, HEAD_DIM)], rows) * scale
            weights = jnp.exp(scores - jnp.max(scores, axis=-1, keepdims=True)).astype(jnp.bfloat16)
            norm = jnp.sum(weights.astype(jnp.float32), axis=-1, keepdims=True)
            out_ref[u, :, pl.ds(h * HEAD_DIM, HEAD_DIM)] = (dot(weights, rows) / norm).astype(jnp.bfloat16)
        return carry

    lax.fori_loop(1, seg_dev, decode_step, 0)
    for copy in behind_stats:
        copy.wait_recv()
    for copy in prior:
        copy.wait_recv()
    total3 = behind2[0]
    for k in range(1, heads_axis):
        total3 = total3 + behind2[k]
    total3 = lax.rsqrt(total3 / full_width + epsilon) * softmax_scale
    key_scale[pl.ds(0, NEIGHBOURS), :] = total3[per_device - NEIGHBOURS:]

    @pl.when(me == 0)
    def _():
        enc[:, pl.ds(0, NEIGHBOURS)] = jnp.zeros((GROUPS, NEIGHBOURS, NBR_LEN, width), jnp.bfloat16)

    decode_step(0, 0)
    for copy in list(sent.values()) + prior + first_stats + second_stats + behind_stats:
        copy.wait_send()


def fused_body(
    neighbour_query,
    neighbour_key,
    neighbour_value,
    segment_key,
    segment_value,
    decoder_query,
    sources,
):
    columns = neighbour_query.shape[1]
    heads_axis = lax.axis_size("head")
    span = lax.axis_size("span")
    per_device = SEG_DEV * NEIGHBOURS
    width = columns // GROUPS
    bf16, f32 = jnp.bfloat16, jnp.float32
    neighbour_shape = (per_device, NBR_LEN, columns)
    segment_shape = (SEG_DEV, SEG_LEN, columns)
    chunks = 2 * GROUPS
    any_space = pl.BlockSpec(memory_space=pl.ANY)
    dma = pltpu.SemaphoreType.DMA
    out = pl.pallas_call(
        functools.partial(kernel, heads_axis, columns * heads_axis),
        out_shape=jax.ShapeDtypeStruct(segment_shape, bf16),
        in_specs=[pl.BlockSpec(memory_space=pltpu.SMEM)] + [any_space] * 6,
        out_specs=pl.BlockSpec(memory_space=pltpu.VMEM),
        scratch_shapes=[pltpu.VMEM(neighbour_shape, bf16)] * 3
        + [pltpu.VMEM(segment_shape, bf16)]
        + [pltpu.VMEM((span * SEG_DEV, SEG_LEN, width), bf16)] * chunks
        + [
            pltpu.VMEM((GROUPS, per_device, NBR_LEN, width), bf16),
            pltpu.VMEM((GROUPS, per_device + NEIGHBOURS, NBR_LEN, width), bf16),
            pltpu.VMEM((per_device, NBR_LEN, HEAD_DIM), f32),
            pltpu.VMEM((per_device, NBR_LEN, NBR_LEN), f32),
            pltpu.VMEM((per_device + NEIGHBOURS, NBR_LEN), f32),
            pltpu.VMEM((per_device, NBR_LEN), f32),
            pltpu.VMEM((per_device, NBR_LEN), f32),
            pltpu.VMEM((heads_axis - 1, per_device, NBR_LEN), f32),
            pltpu.VMEM((heads_axis - 1, per_device, NBR_LEN), f32),
            pltpu.VMEM((heads_axis, per_device, NBR_LEN), f32),
            dma((3, per_device)),
            dma,
            dma((chunks,)),
            dma((8, chunks)),
            dma((8, chunks)),
            dma((3, heads_axis)),
            dma((3, heads_axis)),
            dma((GROUPS,)),
            dma((GROUPS,)),
        ],
        compiler_params=pltpu.CompilerParams(collective_id=0, has_side_effects=True),
    )(
        sources.reshape(per_device),
        neighbour_query.reshape(neighbour_shape),
        neighbour_key.reshape(neighbour_shape),
        neighbour_value.reshape(neighbour_shape),
        segment_key.reshape(segment_shape),
        segment_value.reshape(segment_shape),
        decoder_query.reshape(segment_shape),
    )
    return out.reshape(SEG_DEV * SEG_LEN, columns)


def solution(mesh):
    placed = (
        P("span", "head"),
        P("span", "head"),
        P("span", "head"),
        P("span", "head"),
        P("span", "head"),
        P("span", "head"),
        P("span", None),
    )
    cube = mesh.shape["span"] == 2 * 2 * 2
    return jax.shard_map(
        fused_body if cube else body, mesh=mesh, in_specs=placed, out_specs=P("span", "head"), check_vma=False
    )
```

```python
import functools

import jax
import jax.numpy as jnp
from jax import lax
from jax.experimental import pallas as pl
from jax.experimental.pallas import tpu as pltpu
from jax.sharding import PartitionSpec as P

HEAD_DIM = 128
SEG_LEN = 64
NBR_LEN = 128
NEIGHBOURS = 2
SEG_DEV = 4


epsilon = 1e-06


def from_behind(x, axis, by):
    count = lax.axis_size(axis)
    pairs = [(i, i + by) for i in range(count) if 0 <= i + by < count]
    return lax.ppermute(x, axis, pairs)


def attend(query_rows, key_rows, value_rows):
    groups, length, columns = query_rows.shape
    head_count = columns // HEAD_DIM
    query_heads = query_rows.reshape(groups, length, head_count, HEAD_DIM)
    key_heads = key_rows.reshape(groups, key_rows.shape[1], head_count, HEAD_DIM)
    value_heads = value_rows.reshape(groups, value_rows.shape[1], head_count, HEAD_DIM)
    logit_scores = jnp.einsum(
        "bqhd,bkhd->bhqk", query_heads, key_heads, preferred_element_type=jnp.float32
    ) * HEAD_DIM ** (-0.5)
    logit_scores = logit_scores - jnp.max(logit_scores, axis=-1, keepdims=True)
    weights = jnp.exp(logit_scores)
    weights = (weights / jnp.sum(weights, axis=-1, keepdims=True)).astype(jnp.bfloat16)
    output = jnp.einsum("bhqk,bkhd->bqhd", weights, value_heads, preferred_element_type=jnp.float32)
    return output.reshape(groups, length, columns)


def squares(rows):
    wide = rows.astype(jnp.float32)
    return jnp.sum(wide * wide, axis=-1)


def normalize(rows, totals, full_width):
    scale = lax.rsqrt(totals / full_width + epsilon)
    return (rows.astype(jnp.float32) * scale[:, None]).astype(jnp.bfloat16)


def body(
    neighbour_query,
    neighbour_key,
    neighbour_value,
    segment_key,
    segment_value,
    decoder_query,
    sources,
):
    columns = neighbour_query.shape[1]
    full_width = columns * lax.axis_size("head")
    devices = lax.axis_size("span")
    per_device = SEG_DEV * NEIGHBOURS
    capacity = max(2, 2 * per_device // devices)
    panel_rows = NEIGHBOURS * NBR_LEN
    self_out = attend(
        neighbour_query.reshape(per_device, NBR_LEN, columns),
        neighbour_key.reshape(per_device, NBR_LEN, columns),
        neighbour_value.reshape(per_device, NBR_LEN, columns),
    ).astype(jnp.bfloat16)
    flat_self = self_out.reshape(per_device * NBR_LEN, columns)
    totals = lax.psum(squares(flat_self), "head")
    cross_query = normalize(flat_self, totals, full_width).reshape(per_device, NBR_LEN, columns)
    listed = sources.reshape(per_device)
    owners = listed // SEG_DEV
    within = listed % SEG_DEV
    position = jnp.arange(per_device)
    earlier = (owners[:, None] == owners[None, :]) & (position[:, None] > position[None, :])
    ranked = jnp.sum(earlier.astype(jnp.int32), axis=1)
    slots = owners * capacity + ranked
    picked = (slots[:, None] == jnp.arange(devices * capacity)[None, :]).astype(jnp.int32)
    request = jnp.sum(picked * (within + 1)[:, None], axis=0).reshape(devices, capacity)
    asked = lax.all_to_all(request, "span", split_axis=0, concat_axis=0, tiled=True)
    wanted = jnp.maximum(asked - 1, 0).reshape(devices * capacity)
    own_keys = segment_key.reshape(SEG_DEV, SEG_LEN, columns)[wanted]
    own_values = segment_value.reshape(SEG_DEV, SEG_LEN, columns)[wanted]
    got_keys, got_values = (
        lax.all_to_all(
            own_keys.reshape(devices, capacity, SEG_LEN, columns),
            "span",
            split_axis=0,
            concat_axis=0,
            tiled=True,
        ),
        lax.all_to_all(
            own_values.reshape(devices, capacity, SEG_LEN, columns),
            "span",
            split_axis=0,
            concat_axis=0,
            tiled=True,
        ),
    )
    source_keys = got_keys.reshape(devices * capacity, SEG_LEN, columns)[slots]
    source_values = got_values.reshape(devices * capacity, SEG_LEN, columns)[slots]
    crossed = attend(cross_query, source_keys, source_values).astype(jnp.bfloat16)
    encoded = (self_out.astype(jnp.float32) + crossed.astype(jnp.float32)).astype(jnp.bfloat16)
    encoded = encoded.reshape(per_device * NBR_LEN, columns)
    key_totals = lax.psum(squares(encoded), "head")
    keys_all = normalize(encoded, key_totals, full_width)
    before_keys, before_values = from_behind(
        (keys_all[-panel_rows:], encoded[-panel_rows:]), "span", 1
    )
    used_keys = jnp.concatenate([before_keys, keys_all[:-panel_rows]], axis=0)
    used_values = jnp.concatenate([before_values, encoded[:-panel_rows]], axis=0)
    blended = attend(
        decoder_query.reshape(SEG_DEV, SEG_LEN, columns),
        used_keys.reshape(SEG_DEV, panel_rows, columns),
        used_values.reshape(SEG_DEV, panel_rows, columns),
    ).astype(jnp.bfloat16)
    return blended.reshape(SEG_DEV * SEG_LEN, columns)


MESH = pl.DeviceIdType.MESH
GROUPS = 4


def dot_t(a, b):
    return lax.dot_general(a, b, (((1,), (1,)), ((), ())), preferred_element_type=jnp.float32)


def dot(a, b):
    return lax.dot_general(a, b, (((1,), (0,)), ((), ())), preferred_element_type=jnp.float32)


def kernel(
    heads_axis, full_width,
    src_ref, nq_hbm, nk_hbm, nv_hbm, sk_hbm, sv_hbm, dq_hbm, out_ref,
    nq, nk, nv, dq, *rest,
):
    kbufs, vbufs = rest[:GROUPS], rest[GROUPS:2 * GROUPS]
    (own_out, mixing, enc, squares_acc, row_scale, key_scale,
     stat1, stat2, peer1, peer2, behind2,
     in_sem, dq_sem, local_sem, send_sem, recv_sem,
     stat_send, stat_recv, prior_send, prior_recv) = rest[2 * GROUPS:]
    per_device = nq.shape[0]
    seg_dev = dq.shape[0]
    columns = nq.shape[2]
    width = columns // GROUPS
    group_heads = width // HEAD_DIM
    span = lax.axis_size("span")
    me = lax.axis_index("span")
    lane = lax.axis_index("head")
    core, across, along = me ^ 1, me ^ 2, me ^ 4
    after = lax.rem(me + 1, span)
    before = lax.rem(me + span - 1, span)
    softmax_scale = HEAD_DIM ** (-0.5)

    for i in range(per_device):
        for a, (hbm, vm) in enumerate(((nq_hbm, nq), (nk_hbm, nk), (nv_hbm, nv))):
            pltpu.make_async_copy(hbm.at[i], vm.at[i], in_sem.at[a, i]).start()
    dq_copy = pltpu.make_async_copy(dq_hbm, dq, dq_sem)
    dq_copy.start()

    barrier = pltpu.get_barrier_semaphore()
    greeted = 0
    for target in (core, across, along):
        pl.semaphore_signal(barrier, inc=1, device_id={"span": target, "head": lane}, device_id_type=MESH)
        greeted += 1
    for k in range(1, heads_axis):
        other = lax.rem(lane + k, heads_axis)
        pl.semaphore_signal(barrier, inc=1, device_id={"span": me, "head": other}, device_id_type=MESH)
        greeted += 1
    for k in range(heads_axis):
        other = lax.rem(lane + k, heads_axis)
        for target in (after, before):
            pl.semaphore_signal(barrier, inc=1, device_id={"span": target, "head": other}, device_id_type=MESH)
            greeted += 1
    pl.semaphore_wait(barrier, greeted)

    chunks = 2 * GROUPS

    def buffer(j):
        return (kbufs + vbufs)[j]

    def source(j):
        hbm = (sk_hbm, sv_hbm)[j // GROUPS]
        return hbm.at[:, :, pl.ds((j % GROUPS) * width, width)]

    def block(j, owner):
        return buffer(j).at[pl.ds(owner * seg_dev, seg_dev)]

    def half(j, owner, part):
        rows = seg_dev // 2
        return buffer(j).at[pl.ds(owner * seg_dev + part * rows, rows)]

    sent = {}

    def push(kind, j, src, dst, target):
        copy = pltpu.make_async_remote_copy(
            src_ref=src, dst_ref=dst, send_sem=send_sem.at[kind, j], recv_sem=recv_sem.at[kind, j],
            device_id={"span": target, "head": lane}, device_id_type=MESH)
        copy.start()
        sent[kind, j] = copy

    def direct(j):
        push(0, j, source(j), block(j, me), across)
        push(1, j, source(j), block(j, me), along)

    local = []
    for j in range(chunks):
        direct(j)
        push(4, j, source(j), block(j, me), core)
        copy = pltpu.make_async_copy(source(j), block(j, me), local_sem.at[j])
        copy.start()
        local.append(copy)

    def forward(j):
        sent[2, j].wait_recv()
        sent[3, j].wait_recv()
        push(7, j, block(j, me ^ 6), block(j, me ^ 6), core)

    def step(j):
        sent[1, j].wait_recv()
        push(2, j, half(j, along, 0), half(j, along, 0), across)
        sent[0, j].wait_recv()
        push(3, j, half(j, across, 1), half(j, across, 1), along)
        push(5, j, block(j, across), block(j, across), core)
        push(6, j, block(j, along), block(j, along), core)

    def arrived(j):
        local[j].wait()
        for kind in (4, 5, 6, 7):
            sent[kind, j].wait_recv()

    ones = jnp.ones((NBR_LEN, HEAD_DIM), jnp.bfloat16)

    def self_step(i, carry):
        for a, (hbm, vm) in enumerate(((nq_hbm, nq), (nk_hbm, nk), (nv_hbm, nv))):
            pltpu.make_async_copy(hbm.at[i], vm.at[i], in_sem.at[a, i]).wait()
        total = jnp.zeros((NBR_LEN, HEAD_DIM), jnp.float32)
        for h in range(columns // HEAD_DIM):
            cols = pl.ds(h * HEAD_DIM, HEAD_DIM)
            scores = dot_t(nq[i, :, cols], nk[i, :, cols]) * softmax_scale
            weights = jnp.exp(scores - jnp.max(scores, axis=-1, keepdims=True)).astype(jnp.bfloat16)
            o = (dot(weights, nv[i, :, cols]) / dot(weights, ones)).astype(jnp.bfloat16)
            own_out[h // group_heads, i, :, pl.ds((h % group_heads) * HEAD_DIM, HEAD_DIM)] = o
            wide = o.astype(jnp.float32)
            total = total + wide * wide
        stat1[pl.ds(i, 1), :] = jnp.sum(total.T, axis=0, keepdims=True)
        return carry

    def exchange(kind, stat, peer):
        out = []
        for k in range(1, heads_axis):
            other = lax.rem(lane + k, heads_axis)
            copy = pltpu.make_async_remote_copy(
                src_ref=stat, dst_ref=peer.at[k - 1],
                send_sem=stat_send.at[kind, k - 1], recv_sem=stat_recv.at[kind, k - 1],
                device_id={"span": me, "head": other}, device_id_type=MESH)
            copy.start()
            out.append(copy)
        return out

    def weigh_step(g, i):
        key_rows = kbufs[g][src_ref[i // NEIGHBOURS, i % NEIGHBOURS]]
        scale = row_scale[i, :, :SEG_LEN]
        for h in range(group_heads):
            lo, hi = h * HEAD_DIM, (h + 1) * HEAD_DIM
            scores = dot_t(own_out[g, i, :, pl.ds(lo, HEAD_DIM)], key_rows[:, lo:hi]) * scale
            weights = jnp.exp(scores - jnp.max(scores, axis=-1, keepdims=True))
            weights = weights / jnp.sum(weights, axis=-1, keepdims=True)
            mixing[g, i, h] = weights.astype(jnp.bfloat16)

    def weigh(g):
        arrived(g)

        def pair_step(t, carry):
            for b in range(2):
                weigh_step(g, 2 * t + b)
            return carry

        lax.fori_loop(0, per_device // 2, pair_step, 0)

    def cross_step(g, i):
        value_rows = vbufs[g][src_ref[i // NEIGHBOURS, i % NEIGHBOURS]]
        total = jnp.zeros((NBR_LEN, HEAD_DIM), jnp.float32)
        for h in range(group_heads):
            lo, hi = h * HEAD_DIM, (h + 1) * HEAD_DIM
            first = own_out[g, i, :, pl.ds(lo, HEAD_DIM)]
            crossed = dot(mixing[g, i, h], value_rows[:, lo:hi]).astype(jnp.bfloat16)
            both = (first.astype(jnp.float32) + crossed.astype(jnp.float32)).astype(jnp.bfloat16)
            enc[g, NEIGHBOURS + i, :, pl.ds(lo, HEAD_DIM)] = both
            wide = both.astype(jnp.float32)
            total = total + wide * wide
        if g > 0:
            total = total + squares_acc[i]
        if g < GROUPS - 1:
            squares_acc[i] = total
        else:
            stat2[pl.ds(i, 1), :] = jnp.sum(total.T, axis=0, keepdims=True)

    prior = []

    def cross(g):
        arrived(GROUPS + g)
        for i in range(per_device - NEIGHBOURS, per_device):
            cross_step(g, i)
        copy = pltpu.make_async_remote_copy(
            src_ref=enc.at[g, pl.ds(per_device, NEIGHBOURS)], dst_ref=enc.at[g, pl.ds(0, NEIGHBOURS)],
            send_sem=prior_send.at[g], recv_sem=prior_recv.at[g],
            device_id={"span": after, "head": lane}, device_id_type=MESH)
        copy.start()
        prior.append(copy)

        def rest_step(t, carry):
            for b in range(2):
                cross_step(g, 2 * t + b)
            return carry

        lax.fori_loop(0, (per_device - NEIGHBOURS) // 2, rest_step, 0)

    quarter = per_device // 4
    for j in range(4):
        lax.fori_loop(j * quarter, (j + 1) * quarter, self_step, 0)
        if j > 0:
            step(2 * j - 2)
            step(2 * j - 1)
    first_stats = exchange(0, stat1, peer1)
    step(6)
    for copy in first_stats:
        copy.wait_recv()
    total1 = stat1[...]
    for k in range(heads_axis - 1):
        total1 = total1 + peer1[k]
    total1 = lax.rsqrt(total1 / full_width + epsilon) * softmax_scale
    for i in range(per_device):
        row_scale[i] = jnp.broadcast_to(total1[i:i + 1], (NBR_LEN, NBR_LEN)).T
    step(7)
    forward(0)
    for g in range(GROUPS):
        forward(g + 1)
        weigh(g)
    for g in range(GROUPS):
        if g + 1 < GROUPS:
            forward(GROUPS + 1 + g)
        cross(g)

    second_stats = exchange(1, stat2, peer2)
    behind_stats = []
    for k in range(heads_axis):
        other = lax.rem(lane + k, heads_axis)
        copy = pltpu.make_async_remote_copy(
            src_ref=stat2, dst_ref=behind2.at[k],
            send_sem=stat_send.at[2, k], recv_sem=stat_recv.at[2, k],
            device_id={"span": after, "head": other}, device_id_type=MESH)
        copy.start()
        behind_stats.append(copy)
    dq_copy.wait()
    for copy in second_stats:
        copy.wait_recv()
    total2 = stat2[...]
    for k in range(heads_axis - 1):
        total2 = total2 + peer2[k]
    key_scale[pl.ds(NEIGHBOURS, per_device), :] = lax.rsqrt(total2 / full_width + epsilon) * softmax_scale

    def decode_step(u, carry):
        scales = [key_scale[pl.ds(NEIGHBOURS * u + n, 1), :] for n in range(NEIGHBOURS)]
        scale = jnp.concatenate(scales, axis=1)
        for h in range(columns // HEAD_DIM):
            g, cols = h // group_heads, pl.ds((h % group_heads) * HEAD_DIM, HEAD_DIM)
            rows = enc[g, pl.ds(NEIGHBOURS * u, NEIGHBOURS), :, cols].reshape(NEIGHBOURS * NBR_LEN, HEAD_DIM)
            scores = dot_t(dq[u, :, pl.ds(h * HEAD_DIM, HEAD_DIM)], rows) * scale
            weights = jnp.exp(scores - jnp.max(scores, axis=-1, keepdims=True)).astype(jnp.bfloat16)
            norm = jnp.sum(weights.astype(jnp.float32), axis=-1, keepdims=True)
            out_ref[u, :, pl.ds(h * HEAD_DIM, HEAD_DIM)] = (dot(weights, rows) / norm).astype(jnp.bfloat16)
        return carry

    lax.fori_loop(1, seg_dev, decode_step, 0)
    for copy in behind_stats:
        copy.wait_recv()
    for copy in prior:
        copy.wait_recv()
    total3 = behind2[0]
    for k in range(1, heads_axis):
        total3 = total3 + behind2[k]
    total3 = lax.rsqrt(total3 / full_width + epsilon) * softmax_scale
    key_scale[pl.ds(0, NEIGHBOURS), :] = total3[per_device - NEIGHBOURS:]

    @pl.when(me == 0)
    def _():
        enc[:, pl.ds(0, NEIGHBOURS)] = jnp.zeros((GROUPS, NEIGHBOURS, NBR_LEN, width), jnp.bfloat16)

    decode_step(0, 0)
    for copy in list(sent.values()) + prior + first_stats + second_stats + behind_stats:
        copy.wait_send()


def fused_body(
    neighbour_query,
    neighbour_key,
    neighbour_value,
    segment_key,
    segment_value,
    decoder_query,
    sources,
):
    columns = neighbour_query.shape[1]
    heads_axis = lax.axis_size("head")
    span = lax.axis_size("span")
    per_device = SEG_DEV * NEIGHBOURS
    width = columns // GROUPS
    bf16, f32 = jnp.bfloat16, jnp.float32
    neighbour_shape = (per_device, NBR_LEN, columns)
    segment_shape = (SEG_DEV, SEG_LEN, columns)
    chunks = 2 * GROUPS
    any_space = pl.BlockSpec(memory_space=pltpu.HBM)
    dma = pltpu.SemaphoreType.DMA
    out = pl.pallas_call(
        functools.partial(kernel, heads_axis, columns * heads_axis),
        out_shape=jax.ShapeDtypeStruct(segment_shape, bf16),
        in_specs=[pl.BlockSpec(memory_space=pltpu.SMEM)] + [any_space] * 6,
        out_specs=pl.BlockSpec(memory_space=pltpu.VMEM),
        scratch_shapes=[pltpu.VMEM(neighbour_shape, bf16)] * 3
        + [pltpu.VMEM(segment_shape, bf16)]
        + [pltpu.VMEM((span * SEG_DEV, SEG_LEN, width), bf16)] * chunks
        + [
            pltpu.VMEM((GROUPS, per_device, NBR_LEN, width), bf16),
            pltpu.VMEM((GROUPS, per_device, width // HEAD_DIM, NBR_LEN, SEG_LEN), bf16),
            pltpu.VMEM((GROUPS, per_device + NEIGHBOURS, NBR_LEN, width), bf16),
            pltpu.VMEM((per_device, NBR_LEN, HEAD_DIM), f32),
            pltpu.VMEM((per_device, NBR_LEN, NBR_LEN), f32),
            pltpu.VMEM((per_device + NEIGHBOURS, NBR_LEN), f32),
            pltpu.VMEM((per_device, NBR_LEN), f32),
            pltpu.VMEM((per_device, NBR_LEN), f32),
            pltpu.VMEM((heads_axis - 1, per_device, NBR_LEN), f32),
            pltpu.VMEM((heads_axis - 1, per_device, NBR_LEN), f32),
            pltpu.VMEM((heads_axis, per_device, NBR_LEN), f32),
            dma((3, per_device)),
            dma,
            dma((chunks,)),
            dma((8, chunks)),
            dma((8, chunks)),
            dma((3, heads_axis)),
            dma((3, heads_axis)),
            dma((GROUPS,)),
            dma((GROUPS,)),
        ],
        compiler_params=pltpu.CompilerParams(
            collective_id=0, has_side_effects=True, vmem_limit_bytes=40 * 1024 * 1024),
    )(
        sources,
        neighbour_query.reshape(neighbour_shape),
        neighbour_key.reshape(neighbour_shape),
        neighbour_value.reshape(neighbour_shape),
        segment_key.reshape(segment_shape),
        segment_value.reshape(segment_shape),
        decoder_query.reshape(segment_shape),
    )
    return out.reshape(SEG_DEV * SEG_LEN, columns)


def solution(mesh):
    placed = (
        P("span", "head"),
        P("span", "head"),
        P("span", "head"),
        P("span", "head"),
        P("span", "head"),
        P("span", "head"),
        P("span", None),
    )
    cube = mesh.shape["span"] == 2 * 2 * 2
    return jax.shard_map(
        fused_body if cube else body, mesh=mesh, in_specs=placed, out_specs=P("span", "head"), check_vma=False
    )
```

```python
import functools
import math

import jax
import jax.numpy as jnp
from jax import lax
from jax.experimental import pallas as pl
from jax.experimental.pallas import tpu as pltpu
from jax.sharding import PartitionSpec as P

HEAD_DIM = 128
SEG_LEN = 64
NBR_LEN = 128
NEIGHBOURS = 2
SEG_DEV = 4


epsilon = 1e-06


def from_behind(x, axis, by):
    count = lax.axis_size(axis)
    pairs = [(i, i + by) for i in range(count) if 0 <= i + by < count]
    return lax.ppermute(x, axis, pairs)


def attend(query_rows, key_rows, value_rows):
    groups, length, columns = query_rows.shape
    head_count = columns // HEAD_DIM
    query_heads = query_rows.reshape(groups, length, head_count, HEAD_DIM)
    key_heads = key_rows.reshape(groups, key_rows.shape[1], head_count, HEAD_DIM)
    value_heads = value_rows.reshape(groups, value_rows.shape[1], head_count, HEAD_DIM)
    logit_scores = jnp.einsum(
        "bqhd,bkhd->bhqk", query_heads, key_heads, preferred_element_type=jnp.float32
    ) * HEAD_DIM ** (-0.5)
    logit_scores = logit_scores - jnp.max(logit_scores, axis=-1, keepdims=True)
    weights = jnp.exp(logit_scores)
    weights = (weights / jnp.sum(weights, axis=-1, keepdims=True)).astype(jnp.bfloat16)
    output = jnp.einsum("bhqk,bkhd->bqhd", weights, value_heads, preferred_element_type=jnp.float32)
    return output.reshape(groups, length, columns)


def squares(rows):
    wide = rows.astype(jnp.float32)
    return jnp.sum(wide * wide, axis=-1)


def normalize(rows, totals, full_width):
    scale = lax.rsqrt(totals / full_width + epsilon)
    return (rows.astype(jnp.float32) * scale[:, None]).astype(jnp.bfloat16)


def body(
    neighbour_query,
    neighbour_key,
    neighbour_value,
    segment_key,
    segment_value,
    decoder_query,
    sources,
):
    columns = neighbour_query.shape[1]
    full_width = columns * lax.axis_size("head")
    devices = lax.axis_size("span")
    per_device = SEG_DEV * NEIGHBOURS
    capacity = max(2, 2 * per_device // devices)
    panel_rows = NEIGHBOURS * NBR_LEN
    self_out = attend(
        neighbour_query.reshape(per_device, NBR_LEN, columns),
        neighbour_key.reshape(per_device, NBR_LEN, columns),
        neighbour_value.reshape(per_device, NBR_LEN, columns),
    ).astype(jnp.bfloat16)
    flat_self = self_out.reshape(per_device * NBR_LEN, columns)
    totals = lax.psum(squares(flat_self), "head")
    cross_query = normalize(flat_self, totals, full_width).reshape(per_device, NBR_LEN, columns)
    listed = sources.reshape(per_device)
    owners = listed // SEG_DEV
    within = listed % SEG_DEV
    position = jnp.arange(per_device)
    earlier = (owners[:, None] == owners[None, :]) & (position[:, None] > position[None, :])
    ranked = jnp.sum(earlier.astype(jnp.int32), axis=1)
    slots = owners * capacity + ranked
    picked = (slots[:, None] == jnp.arange(devices * capacity)[None, :]).astype(jnp.int32)
    request = jnp.sum(picked * (within + 1)[:, None], axis=0).reshape(devices, capacity)
    asked = lax.all_to_all(request, "span", split_axis=0, concat_axis=0, tiled=True)
    wanted = jnp.maximum(asked - 1, 0).reshape(devices * capacity)
    own_keys = segment_key.reshape(SEG_DEV, SEG_LEN, columns)[wanted]
    own_values = segment_value.reshape(SEG_DEV, SEG_LEN, columns)[wanted]
    got_keys, got_values = (
        lax.all_to_all(
            own_keys.reshape(devices, capacity, SEG_LEN, columns),
            "span",
            split_axis=0,
            concat_axis=0,
            tiled=True,
        ),
        lax.all_to_all(
            own_values.reshape(devices, capacity, SEG_LEN, columns),
            "span",
            split_axis=0,
            concat_axis=0,
            tiled=True,
        ),
    )
    source_keys = got_keys.reshape(devices * capacity, SEG_LEN, columns)[slots]
    source_values = got_values.reshape(devices * capacity, SEG_LEN, columns)[slots]
    crossed = attend(cross_query, source_keys, source_values).astype(jnp.bfloat16)
    encoded = (self_out.astype(jnp.float32) + crossed.astype(jnp.float32)).astype(jnp.bfloat16)
    encoded = encoded.reshape(per_device * NBR_LEN, columns)
    key_totals = lax.psum(squares(encoded), "head")
    keys_all = normalize(encoded, key_totals, full_width)
    before_keys, before_values = from_behind(
        (keys_all[-panel_rows:], encoded[-panel_rows:]), "span", 1
    )
    used_keys = jnp.concatenate([before_keys, keys_all[:-panel_rows]], axis=0)
    used_values = jnp.concatenate([before_values, encoded[:-panel_rows]], axis=0)
    blended = attend(
        decoder_query.reshape(SEG_DEV, SEG_LEN, columns),
        used_keys.reshape(SEG_DEV, panel_rows, columns),
        used_values.reshape(SEG_DEV, panel_rows, columns),
    ).astype(jnp.bfloat16)
    return blended.reshape(SEG_DEV * SEG_LEN, columns)


MESH = pl.DeviceIdType.MESH
GROUPS = 4


def dot_t(a, b):
    return lax.dot_general(a, b, (((1,), (1,)), ((), ())), preferred_element_type=jnp.float32)


def dot_first(a, b):
    return lax.dot_general(a, b, (((0,), (0,)), ((), ())), preferred_element_type=jnp.float32)


def apart(rows):
    count = rows.shape[1] // HEAD_DIM
    zero = jnp.zeros((rows.shape[0], HEAD_DIM), rows.dtype)
    lines = []
    for h in range(count):
        own = rows[:, h * HEAD_DIM:(h + 1) * HEAD_DIM]
        lines.append(jnp.concatenate([own if k == h else zero for k in range(count)], axis=1))
    return jnp.concatenate(lines, axis=0)


def softmax(scores, axis):
    weights = jnp.exp2(scores - jnp.max(scores, axis=axis, keepdims=True))
    inverse = 1.0 / jnp.sum(weights, axis=axis, keepdims=True)
    return (weights * inverse).astype(jnp.bfloat16)


def kernel(
    heads_axis, full_width,
    src_ref, nq_hbm, nk_hbm, nv_hbm, sk_hbm, sv_hbm, dq_hbm, out_ref,
    nq, nk, nv, dq, *rest,
):
    kbufs, vbufs = rest[:GROUPS], rest[GROUPS:2 * GROUPS]
    (own_out, mixing, enc, squares_acc, row_scale, key_scale,
     stat1, stat2, peer1, peer2, behind2,
     in_sem, dq_sem, local_sem, send_sem, recv_sem,
     stat_send, stat_recv, prior_send, prior_recv) = rest[2 * GROUPS:]
    per_device = nq.shape[0]
    seg_dev = dq.shape[0]
    columns = nq.shape[2]
    width = columns // GROUPS
    group_heads = width // HEAD_DIM
    span = lax.axis_size("span")
    me = lax.axis_index("span")
    lane = lax.axis_index("head")
    core, across, along = me ^ 1, me ^ 2, me ^ 4
    after = lax.rem(me + 1, span)
    before = lax.rem(me + span - 1, span)
    softmax_scale = HEAD_DIM ** (-0.5) / math.log(2.0)

    for i in range(per_device):
        for a, (hbm, vm) in enumerate(((nq_hbm, nq), (nk_hbm, nk), (nv_hbm, nv))):
            pltpu.make_async_copy(hbm.at[i], vm.at[i], in_sem.at[a, i]).start()
    dq_copy = pltpu.make_async_copy(dq_hbm, dq, dq_sem)
    dq_copy.start()

    barrier = pltpu.get_barrier_semaphore()
    greeted = 0
    for target in (core, across, along):
        pl.semaphore_signal(barrier, inc=1, device_id={"span": target, "head": lane}, device_id_type=MESH)
        greeted += 1
    for k in range(1, heads_axis):
        other = lax.rem(lane + k, heads_axis)
        pl.semaphore_signal(barrier, inc=1, device_id={"span": me, "head": other}, device_id_type=MESH)
        greeted += 1
    for k in range(heads_axis):
        other = lax.rem(lane + k, heads_axis)
        for target in (after, before):
            pl.semaphore_signal(barrier, inc=1, device_id={"span": target, "head": other}, device_id_type=MESH)
            greeted += 1
    pl.semaphore_wait(barrier, greeted)

    chunks = 2 * GROUPS

    def buffer(j):
        return (kbufs + vbufs)[j]

    def source(j):
        hbm = (sk_hbm, sv_hbm)[j // GROUPS]
        return hbm.at[:, :, pl.ds((j % GROUPS) * width, width)]

    def block(j, owner):
        return buffer(j).at[pl.ds(owner * seg_dev, seg_dev)]

    def half(j, owner, part):
        rows = seg_dev // 2
        return buffer(j).at[pl.ds(owner * seg_dev + part * rows, rows)]

    sent = {}

    def push(kind, j, src, dst, target):
        copy = pltpu.make_async_remote_copy(
            src_ref=src, dst_ref=dst, send_sem=send_sem.at[kind, j], recv_sem=recv_sem.at[kind, j],
            device_id={"span": target, "head": lane}, device_id_type=MESH)
        copy.start()
        sent[kind, j] = copy

    def direct(j):
        push(0, j, source(j), block(j, me), across)
        push(1, j, source(j), block(j, me), along)

    local = []
    for j in range(chunks):
        direct(j)
        push(4, j, source(j), block(j, me), core)
        copy = pltpu.make_async_copy(source(j), block(j, me), local_sem.at[j])
        copy.start()
        local.append(copy)

    def forward(j):
        sent[2, j].wait_recv()
        sent[3, j].wait_recv()
        push(7, j, block(j, me ^ 6), block(j, me ^ 6), core)

    def step(j):
        sent[1, j].wait_recv()
        push(2, j, half(j, along, 0), half(j, along, 0), across)
        sent[0, j].wait_recv()
        push(3, j, half(j, across, 1), half(j, across, 1), along)
        push(5, j, block(j, across), block(j, across), core)
        push(6, j, block(j, along), block(j, along), core)

    def arrived(j):
        local[j].wait()
        for kind in (4, 5, 6, 7):
            sent[kind, j].wait_recv()

    def self_step(i, carry):
        for a, (hbm, vm) in enumerate(((nq_hbm, nq), (nk_hbm, nk), (nv_hbm, nv))):
            pltpu.make_async_copy(hbm.at[i], vm.at[i], in_sem.at[a, i]).wait()
        total = jnp.zeros((NBR_LEN, HEAD_DIM), jnp.float32)
        for h in range(columns // HEAD_DIM):
            cols = pl.ds(h * HEAD_DIM, HEAD_DIM)
            weights = softmax(dot_t(nk[i, :, cols], nq[i, :, cols]) * softmax_scale, 0)
            o = dot_first(weights, nv[i, :, cols]).astype(jnp.bfloat16)
            own_out[h // group_heads, i, :, pl.ds((h % group_heads) * HEAD_DIM, HEAD_DIM)] = o
            wide = o.astype(jnp.float32)
            total = total + wide * wide
        stat1[pl.ds(i, 1), :] = jnp.sum(total.T, axis=0, keepdims=True)
        return carry

    def exchange(kind, stat, peer):
        out = []
        for k in range(1, heads_axis):
            other = lax.rem(lane + k, heads_axis)
            copy = pltpu.make_async_remote_copy(
                src_ref=stat, dst_ref=peer.at[k - 1],
                send_sem=stat_send.at[kind, k - 1], recv_sem=stat_recv.at[kind, k - 1],
                device_id={"span": me, "head": other}, device_id_type=MESH)
            copy.start()
            out.append(copy)
        return out

    def weigh_step(g, i):
        keys = apart(kbufs[g][src_ref[i // NEIGHBOURS, i % NEIGHBOURS]])
        scores = dot_t(keys, own_out[g, i]) * row_scale[pl.ds(i, 1), :]
        weights = softmax(scores.reshape(group_heads, SEG_LEN, NBR_LEN), 1)
        mixing[g, i] = weights.reshape(group_heads * SEG_LEN, NBR_LEN)

    def weigh(g):
        arrived(g)

        def pair_step(t, carry):
            for b in range(2):
                weigh_step(g, 2 * t + b)
            return carry

        lax.fori_loop(0, per_device // 2, pair_step, 0)

    def cross_step(g, i):
        values = apart(vbufs[g][src_ref[i // NEIGHBOURS, i % NEIGHBOURS]])
        crossed = dot_first(mixing[g, i], values).astype(jnp.bfloat16)
        both = (own_out[g, i].astype(jnp.float32) + crossed.astype(jnp.float32)).astype(jnp.bfloat16)
        enc[g, NEIGHBOURS + i] = both
        wide = both.astype(jnp.float32)
        wide = wide * wide
        total = wide[:, :HEAD_DIM]
        for h in range(1, group_heads):
            total = total + wide[:, h * HEAD_DIM:(h + 1) * HEAD_DIM]
        if g > 0:
            total = total + squares_acc[i]
        if g < GROUPS - 1:
            squares_acc[i] = total
        else:
            stat2[pl.ds(i, 1), :] = jnp.sum(total.T, axis=0, keepdims=True)

    prior = []

    def cross(g):
        arrived(GROUPS + g)
        for i in range(per_device - NEIGHBOURS, per_device):
            cross_step(g, i)
        copy = pltpu.make_async_remote_copy(
            src_ref=enc.at[g, pl.ds(per_device, NEIGHBOURS)], dst_ref=enc.at[g, pl.ds(0, NEIGHBOURS)],
            send_sem=prior_send.at[g], recv_sem=prior_recv.at[g],
            device_id={"span": after, "head": lane}, device_id_type=MESH)
        copy.start()
        prior.append(copy)

        def rest_step(t, carry):
            for b in range(2):
                cross_step(g, 2 * t + b)
            return carry

        lax.fori_loop(0, (per_device - NEIGHBOURS) // 2, rest_step, 0)

    quarter = per_device // 4
    for j in range(4):
        lax.fori_loop(j * quarter, (j + 1) * quarter, self_step, 0)
        if j > 0:
            step(2 * j - 2)
            step(2 * j - 1)
    first_stats = exchange(0, stat1, peer1)
    step(6)
    for copy in first_stats:
        copy.wait_recv()
    total1 = stat1[...]
    for k in range(heads_axis - 1):
        total1 = total1 + peer1[k]
    row_scale[...] = lax.rsqrt(total1 / full_width + epsilon) * softmax_scale
    step(7)
    forward(0)
    for g in range(GROUPS):
        forward(g + 1)
        weigh(g)
    for g in range(GROUPS):
        if g + 1 < GROUPS:
            forward(GROUPS + 1 + g)
        cross(g)

    second_stats = exchange(1, stat2, peer2)
    behind_stats = []
    for k in range(heads_axis):
        other = lax.rem(lane + k, heads_axis)
        copy = pltpu.make_async_remote_copy(
            src_ref=stat2, dst_ref=behind2.at[k],
            send_sem=stat_send.at[2, k], recv_sem=stat_recv.at[2, k],
            device_id={"span": after, "head": other}, device_id_type=MESH)
        copy.start()
        behind_stats.append(copy)
    dq_copy.wait()
    for copy in second_stats:
        copy.wait_recv()
    total2 = stat2[...]
    for k in range(heads_axis - 1):
        total2 = total2 + peer2[k]
    key_scale[pl.ds(NEIGHBOURS, per_device), :] = lax.rsqrt(total2 / full_width + epsilon) * softmax_scale

    def decode_step(u, carry):
        scale = jnp.concatenate([
            jnp.broadcast_to(key_scale[pl.ds(NEIGHBOURS * u + n, 1), :], (NBR_LEN, NBR_LEN)).T
            for n in range(NEIGHBOURS)], axis=0)
        for g in range(GROUPS):
            rows = enc[g, pl.ds(NEIGHBOURS * u, NEIGHBOURS)].reshape(NEIGHBOURS * NBR_LEN, width)
            asked = apart(dq[u, :, pl.ds(g * width, width)])
            out = dot_first(softmax(dot_t(rows, asked) * scale, 0), rows).astype(jnp.bfloat16)
            for h in range(group_heads):
                lo = h * HEAD_DIM
                out_ref[u, :, pl.ds(g * width + lo, HEAD_DIM)] = out[h * SEG_LEN:(h + 1) * SEG_LEN, lo:lo + HEAD_DIM]
        return carry

    lax.fori_loop(1, seg_dev, decode_step, 0)
    for copy in behind_stats:
        copy.wait_recv()
    for copy in prior:
        copy.wait_recv()
    total3 = behind2[0]
    for k in range(1, heads_axis):
        total3 = total3 + behind2[k]
    total3 = lax.rsqrt(total3 / full_width + epsilon) * softmax_scale
    key_scale[pl.ds(0, NEIGHBOURS), :] = total3[per_device - NEIGHBOURS:]

    @pl.when(me == 0)
    def _():
        enc[:, pl.ds(0, NEIGHBOURS)] = jnp.zeros((GROUPS, NEIGHBOURS, NBR_LEN, width), jnp.bfloat16)

    decode_step(0, 0)
    for copy in list(sent.values()) + prior + first_stats + second_stats + behind_stats:
        copy.wait_send()


def fused_body(
    neighbour_query,
    neighbour_key,
    neighbour_value,
    segment_key,
    segment_value,
    decoder_query,
    sources,
):
    columns = neighbour_query.shape[1]
    heads_axis = lax.axis_size("head")
    span = lax.axis_size("span")
    per_device = SEG_DEV * NEIGHBOURS
    width = columns // GROUPS
    bf16, f32 = jnp.bfloat16, jnp.float32
    neighbour_shape = (per_device, NBR_LEN, columns)
    segment_shape = (SEG_DEV, SEG_LEN, columns)
    chunks = 2 * GROUPS
    any_space = pl.BlockSpec(memory_space=pltpu.HBM)
    dma = pltpu.SemaphoreType.DMA
    out = pl.pallas_call(
        functools.partial(kernel, heads_axis, columns * heads_axis),
        out_shape=jax.ShapeDtypeStruct(segment_shape, bf16),
        in_specs=[pl.BlockSpec(memory_space=pltpu.SMEM)] + [any_space] * 6,
        out_specs=pl.BlockSpec(memory_space=pltpu.VMEM),
        scratch_shapes=[pltpu.VMEM(neighbour_shape, bf16)] * 3
        + [pltpu.VMEM(segment_shape, bf16)]
        + [pltpu.VMEM((span * SEG_DEV, SEG_LEN, width), bf16)] * chunks
        + [
            pltpu.VMEM((GROUPS, per_device, NBR_LEN, width), bf16),
            pltpu.VMEM((GROUPS, per_device, width // HEAD_DIM * SEG_LEN, NBR_LEN), bf16),
            pltpu.VMEM((GROUPS, per_device + NEIGHBOURS, NBR_LEN, width), bf16),
            pltpu.VMEM((per_device, NBR_LEN, HEAD_DIM), f32),
            pltpu.VMEM((per_device, NBR_LEN), f32),
            pltpu.VMEM((per_device + NEIGHBOURS, NBR_LEN), f32),
            pltpu.VMEM((per_device, NBR_LEN), f32),
            pltpu.VMEM((per_device, NBR_LEN), f32),
            pltpu.VMEM((heads_axis - 1, per_device, NBR_LEN), f32),
            pltpu.VMEM((heads_axis - 1, per_device, NBR_LEN), f32),
            pltpu.VMEM((heads_axis, per_device, NBR_LEN), f32),
            dma((3, per_device)),
            dma,
            dma((chunks,)),
            dma((8, chunks)),
            dma((8, chunks)),
            dma((3, heads_axis)),
            dma((3, heads_axis)),
            dma((GROUPS,)),
            dma((GROUPS,)),
        ],
        compiler_params=pltpu.CompilerParams(
            collective_id=0, has_side_effects=True, vmem_limit_bytes=53 * 1024 * 1024),
    )(
        sources,
        neighbour_query.reshape(neighbour_shape),
        neighbour_key.reshape(neighbour_shape),
        neighbour_value.reshape(neighbour_shape),
        segment_key.reshape(segment_shape),
        segment_value.reshape(segment_shape),
        decoder_query.reshape(segment_shape),
    )
    return out.reshape(SEG_DEV * SEG_LEN, columns)


def solution(mesh):
    placed = (
        P("span", "head"),
        P("span", "head"),
        P("span", "head"),
        P("span", "head"),
        P("span", "head"),
        P("span", "head"),
        P("span", None),
    )
    cube = mesh.shape["span"] == 2 * 2 * 2
    return jax.shard_map(
        fused_body if cube else body, mesh=mesh, in_specs=placed, out_specs=P("span", "head"), check_vma=False
    )
```

```python
import functools
import math

import jax
import jax.numpy as jnp
from jax import lax
from jax.experimental import pallas as pl
from jax.experimental.pallas import tpu as pltpu
from jax.sharding import PartitionSpec as P

HEAD_DIM = 128
SEG_LEN = 64
NBR_LEN = 128
NEIGHBOURS = 2
SEG_DEV = 4


epsilon = 1e-06


def from_behind(x, axis, by):
    count = lax.axis_size(axis)
    pairs = [(i, i + by) for i in range(count) if 0 <= i + by < count]
    return lax.ppermute(x, axis, pairs)


def attend(query_rows, key_rows, value_rows):
    groups, length, columns = query_rows.shape
    head_count = columns // HEAD_DIM
    query_heads = query_rows.reshape(groups, length, head_count, HEAD_DIM)
    key_heads = key_rows.reshape(groups, key_rows.shape[1], head_count, HEAD_DIM)
    value_heads = value_rows.reshape(groups, value_rows.shape[1], head_count, HEAD_DIM)
    logit_scores = jnp.einsum(
        "bqhd,bkhd->bhqk", query_heads, key_heads, preferred_element_type=jnp.float32
    ) * HEAD_DIM ** (-0.5)
    logit_scores = logit_scores - jnp.max(logit_scores, axis=-1, keepdims=True)
    weights = jnp.exp(logit_scores)
    weights = (weights / jnp.sum(weights, axis=-1, keepdims=True)).astype(jnp.bfloat16)
    output = jnp.einsum("bhqk,bkhd->bqhd", weights, value_heads, preferred_element_type=jnp.float32)
    return output.reshape(groups, length, columns)


def squares(rows):
    wide = rows.astype(jnp.float32)
    return jnp.sum(wide * wide, axis=-1)


def normalize(rows, totals, full_width):
    scale = lax.rsqrt(totals / full_width + epsilon)
    return (rows.astype(jnp.float32) * scale[:, None]).astype(jnp.bfloat16)


def body(
    neighbour_query,
    neighbour_key,
    neighbour_value,
    segment_key,
    segment_value,
    decoder_query,
    sources,
):
    columns = neighbour_query.shape[1]
    full_width = columns * lax.axis_size("head")
    devices = lax.axis_size("span")
    per_device = SEG_DEV * NEIGHBOURS
    capacity = max(2, 2 * per_device // devices)
    panel_rows = NEIGHBOURS * NBR_LEN
    self_out = attend(
        neighbour_query.reshape(per_device, NBR_LEN, columns),
        neighbour_key.reshape(per_device, NBR_LEN, columns),
        neighbour_value.reshape(per_device, NBR_LEN, columns),
    ).astype(jnp.bfloat16)
    flat_self = self_out.reshape(per_device * NBR_LEN, columns)
    totals = lax.psum(squares(flat_self), "head")
    cross_query = normalize(flat_self, totals, full_width).reshape(per_device, NBR_LEN, columns)
    listed = sources.reshape(per_device)
    owners = listed // SEG_DEV
    within = listed % SEG_DEV
    position = jnp.arange(per_device)
    earlier = (owners[:, None] == owners[None, :]) & (position[:, None] > position[None, :])
    ranked = jnp.sum(earlier.astype(jnp.int32), axis=1)
    slots = owners * capacity + ranked
    picked = (slots[:, None] == jnp.arange(devices * capacity)[None, :]).astype(jnp.int32)
    request = jnp.sum(picked * (within + 1)[:, None], axis=0).reshape(devices, capacity)
    asked = lax.all_to_all(request, "span", split_axis=0, concat_axis=0, tiled=True)
    wanted = jnp.maximum(asked - 1, 0).reshape(devices * capacity)
    own_keys = segment_key.reshape(SEG_DEV, SEG_LEN, columns)[wanted]
    own_values = segment_value.reshape(SEG_DEV, SEG_LEN, columns)[wanted]
    got_keys, got_values = (
        lax.all_to_all(
            own_keys.reshape(devices, capacity, SEG_LEN, columns),
            "span",
            split_axis=0,
            concat_axis=0,
            tiled=True,
        ),
        lax.all_to_all(
            own_values.reshape(devices, capacity, SEG_LEN, columns),
            "span",
            split_axis=0,
            concat_axis=0,
            tiled=True,
        ),
    )
    source_keys = got_keys.reshape(devices * capacity, SEG_LEN, columns)[slots]
    source_values = got_values.reshape(devices * capacity, SEG_LEN, columns)[slots]
    crossed = attend(cross_query, source_keys, source_values).astype(jnp.bfloat16)
    encoded = (self_out.astype(jnp.float32) + crossed.astype(jnp.float32)).astype(jnp.bfloat16)
    encoded = encoded.reshape(per_device * NBR_LEN, columns)
    key_totals = lax.psum(squares(encoded), "head")
    keys_all = normalize(encoded, key_totals, full_width)
    before_keys, before_values = from_behind(
        (keys_all[-panel_rows:], encoded[-panel_rows:]), "span", 1
    )
    used_keys = jnp.concatenate([before_keys, keys_all[:-panel_rows]], axis=0)
    used_values = jnp.concatenate([before_values, encoded[:-panel_rows]], axis=0)
    blended = attend(
        decoder_query.reshape(SEG_DEV, SEG_LEN, columns),
        used_keys.reshape(SEG_DEV, panel_rows, columns),
        used_values.reshape(SEG_DEV, panel_rows, columns),
    ).astype(jnp.bfloat16)
    return blended.reshape(SEG_DEV * SEG_LEN, columns)


MESH = pl.DeviceIdType.MESH
GROUPS = 4


def dot_t(a, b):
    return lax.dot_general(a, b, (((1,), (1,)), ((), ())), preferred_element_type=jnp.float32)


def dot_first(a, b):
    return lax.dot_general(a, b, (((0,), (0,)), ((), ())), preferred_element_type=jnp.float32)


def apart(rows):
    count = rows.shape[1] // HEAD_DIM
    zero = jnp.zeros((rows.shape[0], HEAD_DIM), rows.dtype)
    lines = []
    for h in range(count):
        own = rows[:, h * HEAD_DIM:(h + 1) * HEAD_DIM]
        lines.append(jnp.concatenate([own if k == h else zero for k in range(count)], axis=1))
    return jnp.concatenate(lines, axis=0)


def softmax(scores, axis):
    weights = jnp.exp2(scores - jnp.max(scores, axis=axis, keepdims=True))
    inverse = 1.0 / jnp.sum(weights, axis=axis, keepdims=True)
    return (weights * inverse).astype(jnp.bfloat16)


def kernel(
    heads_axis, full_width,
    src_ref, nq_hbm, nk_hbm, nv_hbm, sk_hbm, sv_hbm, dq_hbm, out_ref,
    nq, nk, nv, dq, *rest,
):
    kbufs, vbufs = rest[:GROUPS], rest[GROUPS:2 * GROUPS]
    (own_out, mixing, asked, enc, squares_acc, row_scale, key_scale,
     stat1, stat2, peer1, peer2, behind2,
     in_sem, dq_sem, local_sem, send_sem, recv_sem,
     stat_send, stat_recv, prior_send, prior_recv) = rest[2 * GROUPS:]
    per_device = nq.shape[0]
    seg_dev = dq.shape[0]
    columns = nq.shape[2]
    width = columns // GROUPS
    group_heads = width // HEAD_DIM
    span = lax.axis_size("span")
    me = lax.axis_index("span")
    lane = lax.axis_index("head")
    core, across, along = me ^ 1, me ^ 2, me ^ 4
    after = lax.rem(me + 1, span)
    before = lax.rem(me + span - 1, span)
    softmax_scale = HEAD_DIM ** (-0.5) / math.log(2.0)

    for i in range(per_device):
        for a, (hbm, vm) in enumerate(((nq_hbm, nq), (nk_hbm, nk), (nv_hbm, nv))):
            pltpu.make_async_copy(hbm.at[i], vm.at[i], in_sem.at[a, i]).start()
    dq_copy = pltpu.make_async_copy(dq_hbm, dq, dq_sem)
    dq_copy.start()

    barrier = pltpu.get_barrier_semaphore()
    greeted = 0
    for target in (core, across, along):
        pl.semaphore_signal(barrier, inc=1, device_id={"span": target, "head": lane}, device_id_type=MESH)
        greeted += 1
    for k in range(1, heads_axis):
        other = lax.rem(lane + k, heads_axis)
        pl.semaphore_signal(barrier, inc=1, device_id={"span": me, "head": other}, device_id_type=MESH)
        greeted += 1
    for k in range(heads_axis):
        other = lax.rem(lane + k, heads_axis)
        for target in (after, before):
            pl.semaphore_signal(barrier, inc=1, device_id={"span": target, "head": other}, device_id_type=MESH)
            greeted += 1
    pl.semaphore_wait(barrier, greeted)

    chunks = 2 * GROUPS

    def buffer(j):
        return (kbufs + vbufs)[j]

    def source(j):
        hbm = (sk_hbm, sv_hbm)[j // GROUPS]
        return hbm.at[:, :, pl.ds((j % GROUPS) * width, width)]

    def block(j, owner):
        return buffer(j).at[pl.ds(owner * seg_dev, seg_dev)]

    def half(j, owner, part):
        rows = seg_dev // 2
        return buffer(j).at[pl.ds(owner * seg_dev + part * rows, rows)]

    sent = {}

    def push(kind, j, src, dst, target):
        copy = pltpu.make_async_remote_copy(
            src_ref=src, dst_ref=dst, send_sem=send_sem.at[kind, j], recv_sem=recv_sem.at[kind, j],
            device_id={"span": target, "head": lane}, device_id_type=MESH)
        copy.start()
        sent[kind, j] = copy

    def direct(j):
        push(0, j, source(j), block(j, me), across)
        push(1, j, source(j), block(j, me), along)

    local = []
    for j in range(chunks):
        direct(j)
        push(4, j, source(j), block(j, me), core)
        copy = pltpu.make_async_copy(source(j), block(j, me), local_sem.at[j])
        copy.start()
        local.append(copy)

    def forward(j):
        for part in range(2):
            sent[2 + part, j].wait_recv()
            push(7 + part, j, half(j, me ^ 6, part), half(j, me ^ 6, part), core)

    def step(j):
        sent[1, j].wait_recv()
        push(2, j, half(j, along, 0), half(j, along, 0), across)
        sent[0, j].wait_recv()
        push(3, j, half(j, across, 1), half(j, across, 1), along)
        push(5, j, block(j, across), block(j, across), core)
        push(6, j, block(j, along), block(j, along), core)

    def arrived(j):
        local[j].wait()
        for kind in (4, 5, 6, 7, 8):
            sent[kind, j].wait_recv()

    def self_step(i, carry):
        for a, (hbm, vm) in enumerate(((nq_hbm, nq), (nk_hbm, nk), (nv_hbm, nv))):
            pltpu.make_async_copy(hbm.at[i], vm.at[i], in_sem.at[a, i]).wait()
        total = jnp.zeros((NBR_LEN, HEAD_DIM), jnp.float32)
        for base in range(0, columns // HEAD_DIM, 8):
            together = range(base, base + 8)
            cols = [pl.ds(h * HEAD_DIM, HEAD_DIM) for h in together]
            scores = [dot_t(nk[i, :, c], nq[i, :, c]) * softmax_scale for c in cols]
            weights = [softmax(x, 0) for x in scores]
            outs = [dot_first(w, nv[i, :, c]).astype(jnp.bfloat16) for w, c in zip(weights, cols)]
            for h, o in zip(together, outs):
                own_out[h // group_heads, i, :, pl.ds((h % group_heads) * HEAD_DIM, HEAD_DIM)] = o
                wide = o.astype(jnp.float32)
                total = total + wide * wide
        stat1[pl.ds(i, 1), :] = jnp.sum(total.T, axis=0, keepdims=True)
        return carry

    def exchange(kind, stat, peer):
        out = []
        for k in range(1, heads_axis):
            other = lax.rem(lane + k, heads_axis)
            copy = pltpu.make_async_remote_copy(
                src_ref=stat, dst_ref=peer.at[k - 1],
                send_sem=stat_send.at[kind, k - 1], recv_sem=stat_recv.at[kind, k - 1],
                device_id={"span": me, "head": other}, device_id_type=MESH)
            copy.start()
            out.append(copy)
        return out

    def weigh(g):
        arrived(g)

        def some(t, carry):
            rows = [4 * t + b for b in range(4)]
            keys = [apart(kbufs[g][src_ref[i % NEIGHBOURS, i // NEIGHBOURS]]) for i in rows]
            scores = [dot_t(k, own_out[g, i]) * row_scale[pl.ds(i, 1), :] for k, i in zip(keys, rows)]
            weights = [softmax(x.reshape(group_heads, SEG_LEN, NBR_LEN), 1) for x in scores]
            for i, w in zip(rows, weights):
                mixing[g, i] = w.reshape(group_heads * SEG_LEN, NBR_LEN)
            return carry

        lax.fori_loop(0, per_device // 4, some, 0)

    def cross_rows(g, rows):
        values = [apart(vbufs[g][src_ref[i % NEIGHBOURS, i // NEIGHBOURS]]) for i in rows]
        crossed = [dot_first(mixing[g, i], v).astype(jnp.bfloat16) for i, v in zip(rows, values)]
        for i, x in zip(rows, crossed):
            both = (own_out[g, i].astype(jnp.float32) + x.astype(jnp.float32)).astype(jnp.bfloat16)
            enc[g, NEIGHBOURS + i] = both
            wide = both.astype(jnp.float32)
            wide = wide * wide
            total = wide[:, :HEAD_DIM]
            for h in range(1, group_heads):
                total = total + wide[:, h * HEAD_DIM:(h + 1) * HEAD_DIM]
            if g > 0:
                total = total + squares_acc[i]
            if g < GROUPS - 1:
                squares_acc[i] = total
            else:
                stat2[pl.ds(i, 1), :] = jnp.sum(total.T, axis=0, keepdims=True)

    prior = []

    def panel(g, u):
        return enc[g, pl.ds(NEIGHBOURS * u, NEIGHBOURS)].reshape(NEIGHBOURS * NBR_LEN, width)

    def ask(g, u):
        asked[u, g] = dot_t(panel(g, u), apart(dq[u, :, pl.ds(g * width, width)]))

    def cross(g):
        arrived(GROUPS + g)
        cross_rows(g, list(range(per_device - NEIGHBOURS, per_device)))
        copy = pltpu.make_async_remote_copy(
            src_ref=enc.at[g, pl.ds(per_device, NEIGHBOURS)], dst_ref=enc.at[g, pl.ds(0, NEIGHBOURS)],
            send_sem=prior_send.at[g], recv_sem=prior_recv.at[g],
            device_id={"span": after, "head": lane}, device_id_type=MESH)
        copy.start()
        prior.append(copy)

        def rest_step(t, carry):
            cross_rows(g, [3 * t + b for b in range(3)])
            return carry

        lax.fori_loop(0, (per_device - NEIGHBOURS) // 3, rest_step, 0)

    quarter = per_device // 4
    for j in range(4):
        lax.fori_loop(j * quarter, (j + 1) * quarter, self_step, 0)
        if j > 0:
            step(2 * j - 2)
            step(2 * j - 1)
    first_stats = exchange(0, stat1, peer1)
    step(6)
    for copy in first_stats:
        copy.wait_recv()
    total1 = stat1[...]
    for k in range(heads_axis - 1):
        total1 = total1 + peer1[k]
    row_scale[...] = lax.rsqrt(total1 / full_width + epsilon) * softmax_scale
    step(7)
    forward(0)
    for g in range(GROUPS):
        forward(g + 1)
        weigh(g)
    dq_copy.wait()
    for g in range(GROUPS):
        if g + 1 < GROUPS:
            forward(GROUPS + 1 + g)
        cross(g)
        if g + 1 < GROUPS:
            for u in range(1, seg_dev):
                ask(g, u)

    second_stats = exchange(1, stat2, peer2)
    behind_stats = []
    for k in range(heads_axis):
        other = lax.rem(lane + k, heads_axis)
        copy = pltpu.make_async_remote_copy(
            src_ref=stat2, dst_ref=behind2.at[k],
            send_sem=stat_send.at[2, k], recv_sem=stat_recv.at[2, k],
            device_id={"span": after, "head": other}, device_id_type=MESH)
        copy.start()
        behind_stats.append(copy)
    for u in range(1, seg_dev):
        ask(GROUPS - 1, u)
    for copy in second_stats:
        copy.wait_recv()
    total2 = stat2[...]
    for k in range(heads_axis - 1):
        total2 = total2 + peer2[k]
    key_scale[pl.ds(NEIGHBOURS, per_device), :] = lax.rsqrt(total2 / full_width + epsilon) * softmax_scale

    def decode_step(u, carry):
        scale = jnp.concatenate([
            jnp.broadcast_to(key_scale[pl.ds(NEIGHBOURS * u + n, 1), :], (NBR_LEN, NBR_LEN)).T
            for n in range(NEIGHBOURS)], axis=0)
        weights = [softmax(asked[u, g] * scale, 0) for g in range(GROUPS)]
        outs = [dot_first(w, panel(g, u)).astype(jnp.bfloat16) for g, w in enumerate(weights)]
        for g, out in enumerate(outs):
            for h in range(group_heads):
                lo = h * HEAD_DIM
                out_ref[u, :, pl.ds(g * width + lo, HEAD_DIM)] = out[h * SEG_LEN:(h + 1) * SEG_LEN, lo:lo + HEAD_DIM]
        return carry

    lax.fori_loop(1, seg_dev, decode_step, 0)
    for copy in behind_stats:
        copy.wait_recv()
    for copy in prior:
        copy.wait_recv()
    total3 = behind2[0]
    for k in range(1, heads_axis):
        total3 = total3 + behind2[k]
    total3 = lax.rsqrt(total3 / full_width + epsilon) * softmax_scale
    key_scale[pl.ds(0, NEIGHBOURS), :] = total3[per_device - NEIGHBOURS:]

    @pl.when(me == 0)
    def _():
        enc[:, pl.ds(0, NEIGHBOURS)] = jnp.zeros((GROUPS, NEIGHBOURS, NBR_LEN, width), jnp.bfloat16)

    for g in range(GROUPS):
        ask(g, 0)
    decode_step(0, 0)
    for copy in list(sent.values()) + prior + first_stats + second_stats + behind_stats:
        copy.wait_send()


def fused_body(
    neighbour_query,
    neighbour_key,
    neighbour_value,
    segment_key,
    segment_value,
    decoder_query,
    sources,
):
    columns = neighbour_query.shape[1]
    heads_axis = lax.axis_size("head")
    span = lax.axis_size("span")
    per_device = SEG_DEV * NEIGHBOURS
    width = columns // GROUPS
    bf16, f32 = jnp.bfloat16, jnp.float32
    neighbour_shape = (per_device, NBR_LEN, columns)
    segment_shape = (SEG_DEV, SEG_LEN, columns)
    chunks = 2 * GROUPS
    any_space = pl.BlockSpec(memory_space=pltpu.HBM)
    dma = pltpu.SemaphoreType.DMA
    out = pl.pallas_call(
        functools.partial(kernel, heads_axis, columns * heads_axis),
        out_shape=jax.ShapeDtypeStruct(segment_shape, bf16),
        in_specs=[pl.BlockSpec(memory_space=pltpu.SMEM)] + [any_space] * 6,
        out_specs=pl.BlockSpec(memory_space=pltpu.VMEM),
        scratch_shapes=[pltpu.VMEM(neighbour_shape, bf16)] * 3
        + [pltpu.VMEM(segment_shape, bf16)]
        + [pltpu.VMEM((span * SEG_DEV, SEG_LEN, width), bf16)] * chunks
        + [
            pltpu.VMEM((GROUPS, per_device, NBR_LEN, width), bf16),
            pltpu.VMEM((GROUPS, per_device, width // HEAD_DIM * SEG_LEN, NBR_LEN), bf16),
            pltpu.VMEM((SEG_DEV, GROUPS, NEIGHBOURS * NBR_LEN, width // HEAD_DIM * SEG_LEN), f32),
            pltpu.VMEM((GROUPS, per_device + NEIGHBOURS, NBR_LEN, width), bf16),
            pltpu.VMEM((per_device, NBR_LEN, HEAD_DIM), f32),
            pltpu.VMEM((per_device, NBR_LEN), f32),
            pltpu.VMEM((per_device + NEIGHBOURS, NBR_LEN), f32),
            pltpu.VMEM((per_device, NBR_LEN), f32),
            pltpu.VMEM((per_device, NBR_LEN), f32),
            pltpu.VMEM((heads_axis - 1, per_device, NBR_LEN), f32),
            pltpu.VMEM((heads_axis - 1, per_device, NBR_LEN), f32),
            pltpu.VMEM((heads_axis, per_device, NBR_LEN), f32),
            dma((3, per_device)),
            dma,
            dma((chunks,)),
            dma((9, chunks)),
            dma((9, chunks)),
            dma((3, heads_axis)),
            dma((3, heads_axis)),
            dma((GROUPS,)),
            dma((GROUPS,)),
        ],
        compiler_params=pltpu.CompilerParams(
            collective_id=0, has_side_effects=True, vmem_limit_bytes=53 * 1024 * 1024),
    )(
        sources.T,
        neighbour_query.reshape(neighbour_shape),
        neighbour_key.reshape(neighbour_shape),
        neighbour_value.reshape(neighbour_shape),
        segment_key.reshape(segment_shape),
        segment_value.reshape(segment_shape),
        decoder_query.reshape(segment_shape),
    )
    return out.reshape(SEG_DEV * SEG_LEN, columns)


def solution(mesh):
    placed = (
        P("span", "head"),
        P("span", "head"),
        P("span", "head"),
        P("span", "head"),
        P("span", "head"),
        P("span", "head"),
        P("span", None),
    )
    cube = mesh.shape["span"] == 2 * 2 * 2
    return jax.shard_map(
        fused_body if cube else body, mesh=mesh, in_specs=placed, out_specs=P("span", "head"), check_vma=False
    )
```

```python
import functools
import math

import jax
import jax.numpy as jnp
from jax import lax
from jax.experimental import pallas as pl
from jax.experimental.pallas import tpu as pltpu
from jax.sharding import PartitionSpec as P

HEAD_DIM = 128
SEG_LEN = 64
NBR_LEN = 128
NEIGHBOURS = 2
SEG_DEV = 4


epsilon = 1e-06


def from_behind(x, axis, by):
    count = lax.axis_size(axis)
    pairs = [(i, i + by) for i in range(count) if 0 <= i + by < count]
    return lax.ppermute(x, axis, pairs)


def attend(query_rows, key_rows, value_rows):
    groups, length, columns = query_rows.shape
    head_count = columns // HEAD_DIM
    query_heads = query_rows.reshape(groups, length, head_count, HEAD_DIM)
    key_heads = key_rows.reshape(groups, key_rows.shape[1], head_count, HEAD_DIM)
    value_heads = value_rows.reshape(groups, value_rows.shape[1], head_count, HEAD_DIM)
    logit_scores = jnp.einsum(
        "bqhd,bkhd->bhqk", query_heads, key_heads, preferred_element_type=jnp.float32
    ) * HEAD_DIM ** (-0.5)
    logit_scores = logit_scores - jnp.max(logit_scores, axis=-1, keepdims=True)
    weights = jnp.exp(logit_scores)
    weights = (weights / jnp.sum(weights, axis=-1, keepdims=True)).astype(jnp.bfloat16)
    output = jnp.einsum("bhqk,bkhd->bqhd", weights, value_heads, preferred_element_type=jnp.float32)
    return output.reshape(groups, length, columns)


def squares(rows):
    wide = rows.astype(jnp.float32)
    return jnp.sum(wide * wide, axis=-1)


def normalize(rows, totals, full_width):
    scale = lax.rsqrt(totals / full_width + epsilon)
    return (rows.astype(jnp.float32) * scale[:, None]).astype(jnp.bfloat16)


def body(
    neighbour_query,
    neighbour_key,
    neighbour_value,
    segment_key,
    segment_value,
    decoder_query,
    sources,
):
    columns = neighbour_query.shape[1]
    full_width = columns * lax.axis_size("head")
    devices = lax.axis_size("span")
    per_device = SEG_DEV * NEIGHBOURS
    capacity = max(2, 2 * per_device // devices)
    panel_rows = NEIGHBOURS * NBR_LEN
    self_out = attend(
        neighbour_query.reshape(per_device, NBR_LEN, columns),
        neighbour_key.reshape(per_device, NBR_LEN, columns),
        neighbour_value.reshape(per_device, NBR_LEN, columns),
    ).astype(jnp.bfloat16)
    flat_self = self_out.reshape(per_device * NBR_LEN, columns)
    totals = lax.psum(squares(flat_self), "head")
    cross_query = normalize(flat_self, totals, full_width).reshape(per_device, NBR_LEN, columns)
    listed = sources.reshape(per_device)
    owners = listed // SEG_DEV
    within = listed % SEG_DEV
    position = jnp.arange(per_device)
    earlier = (owners[:, None] == owners[None, :]) & (position[:, None] > position[None, :])
    ranked = jnp.sum(earlier.astype(jnp.int32), axis=1)
    slots = owners * capacity + ranked
    picked = (slots[:, None] == jnp.arange(devices * capacity)[None, :]).astype(jnp.int32)
    request = jnp.sum(picked * (within + 1)[:, None], axis=0).reshape(devices, capacity)
    asked = lax.all_to_all(request, "span", split_axis=0, concat_axis=0, tiled=True)
    wanted = jnp.maximum(asked - 1, 0).reshape(devices * capacity)
    own_keys = segment_key.reshape(SEG_DEV, SEG_LEN, columns)[wanted]
    own_values = segment_value.reshape(SEG_DEV, SEG_LEN, columns)[wanted]
    got_keys, got_values = (
        lax.all_to_all(
            own_keys.reshape(devices, capacity, SEG_LEN, columns),
            "span",
            split_axis=0,
            concat_axis=0,
            tiled=True,
        ),
        lax.all_to_all(
            own_values.reshape(devices, capacity, SEG_LEN, columns),
            "span",
            split_axis=0,
            concat_axis=0,
            tiled=True,
        ),
    )
    source_keys = got_keys.reshape(devices * capacity, SEG_LEN, columns)[slots]
    source_values = got_values.reshape(devices * capacity, SEG_LEN, columns)[slots]
    crossed = attend(cross_query, source_keys, source_values).astype(jnp.bfloat16)
    encoded = (self_out.astype(jnp.float32) + crossed.astype(jnp.float32)).astype(jnp.bfloat16)
    encoded = encoded.reshape(per_device * NBR_LEN, columns)
    key_totals = lax.psum(squares(encoded), "head")
    keys_all = normalize(encoded, key_totals, full_width)
    before_keys, before_values = from_behind(
        (keys_all[-panel_rows:], encoded[-panel_rows:]), "span", 1
    )
    used_keys = jnp.concatenate([before_keys, keys_all[:-panel_rows]], axis=0)
    used_values = jnp.concatenate([before_values, encoded[:-panel_rows]], axis=0)
    blended = attend(
        decoder_query.reshape(SEG_DEV, SEG_LEN, columns),
        used_keys.reshape(SEG_DEV, panel_rows, columns),
        used_values.reshape(SEG_DEV, panel_rows, columns),
    ).astype(jnp.bfloat16)
    return blended.reshape(SEG_DEV * SEG_LEN, columns)


MESH = pl.DeviceIdType.MESH
GROUPS = 4


def dot_t(a, b):
    return lax.dot_general(a, b, (((1,), (1,)), ((), ())), preferred_element_type=jnp.float32)


def dot_first(a, b):
    return lax.dot_general(a, b, (((0,), (0,)), ((), ())), preferred_element_type=jnp.float32)


def apart(rows):
    count = rows.shape[1] // HEAD_DIM
    zero = jnp.zeros((rows.shape[0], HEAD_DIM), rows.dtype)
    lines = []
    for h in range(count):
        own = rows[:, h * HEAD_DIM:(h + 1) * HEAD_DIM]
        lines.append(jnp.concatenate([own if k == h else zero for k in range(count)], axis=1))
    return jnp.concatenate(lines, axis=0)


def softmax(scores, axis):
    weights = jnp.exp2(scores - jnp.max(scores, axis=axis, keepdims=True))
    inverse = 1.0 / jnp.sum(weights, axis=axis, keepdims=True)
    return (weights * inverse).astype(jnp.bfloat16)


def kernel(
    heads_axis, full_width,
    src_ref, nq_hbm, nk_hbm, nv_hbm, sk_hbm, sv_hbm, dq_hbm, out_ref,
    nq, nk, nv, dq, *rest,
):
    kbufs, vbufs = rest[:GROUPS], rest[GROUPS:2 * GROUPS]
    (own_out, mixing, asked, enc, squares_acc, row_scale, key_scale,
     stat1, stat2, peer1, peer2, behind2,
     in_sem, dq_sem, local_sem, send_sem, recv_sem,
     stat_send, stat_recv, prior_send, prior_recv) = rest[2 * GROUPS:]
    per_device = nq.shape[0]
    seg_dev = dq.shape[0]
    columns = nq.shape[2]
    width = columns // GROUPS
    group_heads = width // HEAD_DIM
    span = lax.axis_size("span")
    me = lax.axis_index("span")
    lane = lax.axis_index("head")
    core, across, along = me ^ 1, me ^ 2, me ^ 4
    after = lax.rem(me + 1, span)
    before = lax.rem(me + span - 1, span)
    softmax_scale = HEAD_DIM ** (-0.5) / math.log(2.0)

    barrier = pltpu.get_barrier_semaphore()
    greeted = 0
    for target in (core, across, along):
        pl.semaphore_signal(barrier, inc=1, device_id={"span": target, "head": lane}, device_id_type=MESH)
        greeted += 1
    for k in range(1, heads_axis):
        other = lax.rem(lane + k, heads_axis)
        pl.semaphore_signal(barrier, inc=1, device_id={"span": me, "head": other}, device_id_type=MESH)
        greeted += 1
    for target in (after, before):
        pl.semaphore_signal(barrier, inc=1, device_id={"span": target, "head": lane}, device_id_type=MESH)
        greeted += 1
    pl.semaphore_wait(barrier, greeted)

    chunks = 2 * GROUPS

    def buffer(j):
        return (kbufs + vbufs)[j]

    def source(j):
        hbm = (sk_hbm, sv_hbm)[j // GROUPS]
        return hbm.at[:, :, pl.ds((j % GROUPS) * width, width)]

    def block(j, owner):
        return buffer(j).at[pl.ds(owner * seg_dev, seg_dev)]

    def half(j, owner, part):
        rows = seg_dev // 2
        return buffer(j).at[pl.ds(owner * seg_dev + part * rows, rows)]

    sent = {}

    def push(kind, j, src, dst, target):
        copy = pltpu.make_async_remote_copy(
            src_ref=src, dst_ref=dst, send_sem=send_sem.at[kind, j], recv_sem=recv_sem.at[kind, j],
            device_id={"span": target, "head": lane}, device_id_type=MESH)
        copy.start()
        sent[kind, j] = copy

    def direct(j):
        push(0, j, source(j), block(j, me), across)
        push(1, j, source(j), block(j, me), along)

    local = []
    for j in range(chunks):
        direct(j)

    for i in range(per_device):
        for a, (hbm, vm) in enumerate(((nq_hbm, nq), (nk_hbm, nk), (nv_hbm, nv))):
            pltpu.make_async_copy(hbm.at[i], vm.at[i], in_sem.at[a, i]).start()
    dq_copy = pltpu.make_async_copy(dq_hbm, dq, dq_sem)
    dq_copy.start()

    for j in range(chunks):
        push(4, j, source(j), block(j, me), core)
        copy = pltpu.make_async_copy(source(j), block(j, me), local_sem.at[j])
        copy.start()
        local.append(copy)

    def forward(j):
        for part in range(2):
            sent[2 + part, j].wait_recv()
            push(7 + part, j, half(j, me ^ 6, part), half(j, me ^ 6, part), core)

    def step(j):
        sent[1, j].wait_recv()
        push(2, j, half(j, along, 0), half(j, along, 0), across)
        sent[0, j].wait_recv()
        push(3, j, half(j, across, 1), half(j, across, 1), along)
        push(5, j, block(j, across), block(j, across), core)
        push(6, j, block(j, along), block(j, along), core)

    def arrived(j):
        local[j].wait()
        for kind in (4, 5, 6, 7, 8):
            sent[kind, j].wait_recv()

    def self_step(i, carry):
        for a, (hbm, vm) in enumerate(((nq_hbm, nq), (nk_hbm, nk), (nv_hbm, nv))):
            pltpu.make_async_copy(hbm.at[i], vm.at[i], in_sem.at[a, i]).wait()
        total = jnp.zeros((NBR_LEN, HEAD_DIM), jnp.float32)
        for base in range(0, columns // HEAD_DIM, 8):
            together = range(base, base + 8)
            cols = [pl.ds(h * HEAD_DIM, HEAD_DIM) for h in together]
            scores = [dot_t(nk[i, :, c], nq[i, :, c]) * softmax_scale for c in cols]
            weights = [softmax(x, 0) for x in scores]
            outs = [dot_first(w, nv[i, :, c]).astype(jnp.bfloat16) for w, c in zip(weights, cols)]
            for h, o in zip(together, outs):
                own_out[h // group_heads, i, :, pl.ds((h % group_heads) * HEAD_DIM, HEAD_DIM)] = o
                wide = o.astype(jnp.float32)
                total = total + wide * wide
        stat1[pl.ds(i, 1), :] = jnp.sum(total.T, axis=0, keepdims=True)
        return carry

    def exchange(kind, stat, peer):
        out = []
        for k in range(1, heads_axis):
            other = lax.rem(lane + k, heads_axis)
            copy = pltpu.make_async_remote_copy(
                src_ref=stat, dst_ref=peer.at[k - 1],
                send_sem=stat_send.at[kind, k - 1], recv_sem=stat_recv.at[kind, k - 1],
                device_id={"span": me, "head": other}, device_id_type=MESH)
            copy.start()
            out.append(copy)
        return out

    def weigh(g):
        arrived(g)

        def some(t, carry):
            rows = [4 * t + b for b in range(4)]
            keys = [apart(kbufs[g][src_ref[i % NEIGHBOURS, i // NEIGHBOURS]]) for i in rows]
            scores = [dot_t(k, own_out[g, i]) * row_scale[pl.ds(i, 1), :] for k, i in zip(keys, rows)]
            weights = [softmax(x.reshape(group_heads, SEG_LEN, NBR_LEN), 1) for x in scores]
            for i, w in zip(rows, weights):
                mixing[g, i] = w.reshape(group_heads * SEG_LEN, NBR_LEN)
            return carry

        lax.fori_loop(0, per_device // 4, some, 0)

    def cross_rows(g, rows):
        values = [apart(vbufs[g][src_ref[i % NEIGHBOURS, i // NEIGHBOURS]]) for i in rows]
        crossed = [dot_first(mixing[g, i], v).astype(jnp.bfloat16) for i, v in zip(rows, values)]
        for i, x in zip(rows, crossed):
            both = (own_out[g, i].astype(jnp.float32) + x.astype(jnp.float32)).astype(jnp.bfloat16)
            enc[g, NEIGHBOURS + i] = both
            wide = both.astype(jnp.float32)
            wide = wide * wide
            total = wide[:, :HEAD_DIM]
            for h in range(1, group_heads):
                total = total + wide[:, h * HEAD_DIM:(h + 1) * HEAD_DIM]
            if g > 0:
                total = total + squares_acc[i]
            if g < GROUPS - 1:
                squares_acc[i] = total
            else:
                stat2[pl.ds(i, 1), :] = jnp.sum(total.T, axis=0, keepdims=True)

    prior = []

    def panel(g, u):
        return enc[g, pl.ds(NEIGHBOURS * u, NEIGHBOURS)].reshape(NEIGHBOURS * NBR_LEN, width)

    def ask(g, u):
        asked[u, g] = dot_t(panel(g, u), apart(dq[u, :, pl.ds(g * width, width)]))

    def cross(g):
        arrived(GROUPS + g)
        cross_rows(g, list(range(per_device - NEIGHBOURS, per_device)))
        copy = pltpu.make_async_remote_copy(
            src_ref=enc.at[g, pl.ds(per_device, NEIGHBOURS)], dst_ref=enc.at[g, pl.ds(0, NEIGHBOURS)],
            send_sem=prior_send.at[g], recv_sem=prior_recv.at[g],
            device_id={"span": after, "head": lane}, device_id_type=MESH)
        copy.start()
        prior.append(copy)

        def rest_step(t, carry):
            cross_rows(g, [3 * t + b for b in range(3)])
            return carry

        lax.fori_loop(0, (per_device - NEIGHBOURS) // 3, rest_step, 0)

    quarter = per_device // 4
    for j in range(4):
        lax.fori_loop(j * quarter, (j + 1) * quarter, self_step, 0)
        if j > 0:
            step(2 * j - 2)
            step(2 * j - 1)
    first_stats = exchange(0, stat1, peer1)
    step(6)
    for copy in first_stats:
        copy.wait_recv()
    total1 = stat1[...]
    for k in range(heads_axis - 1):
        total1 = total1 + peer1[k]
    row_scale[...] = lax.rsqrt(total1 / full_width + epsilon) * softmax_scale
    step(7)
    forward(0)
    for g in range(GROUPS):
        forward(g + 1)
        weigh(g)
    dq_copy.wait()
    for g in range(GROUPS):
        if g + 1 < GROUPS:
            forward(GROUPS + 1 + g)
        cross(g)
        if g + 1 < GROUPS:
            for u in range(1, seg_dev):
                ask(g, u)

    second_stats = exchange(1, stat2, peer2)
    handed = pltpu.make_async_remote_copy(
        src_ref=stat2, dst_ref=behind2.at[0],
        send_sem=stat_send.at[2, 0], recv_sem=stat_recv.at[2, 0],
        device_id={"span": after, "head": lane}, device_id_type=MESH)
    handed.start()
    for u in range(1, seg_dev):
        ask(GROUPS - 1, u)
    handed.wait_recv()
    behind_stats = []
    for k in range(1, heads_axis):
        other = lax.rem(lane + k, heads_axis)
        copy = pltpu.make_async_remote_copy(
            src_ref=behind2.at[0], dst_ref=behind2.at[k],
            send_sem=stat_send.at[2, k], recv_sem=stat_recv.at[2, k],
            device_id={"span": me, "head": other}, device_id_type=MESH)
        copy.start()
        behind_stats.append(copy)
    for copy in second_stats:
        copy.wait_recv()
    total2 = stat2[...]
    for k in range(heads_axis - 1):
        total2 = total2 + peer2[k]
    key_scale[pl.ds(NEIGHBOURS, per_device), :] = lax.rsqrt(total2 / full_width + epsilon) * softmax_scale

    def decode_step(u, carry):
        scale = jnp.concatenate([
            jnp.broadcast_to(key_scale[pl.ds(NEIGHBOURS * u + n, 1), :], (NBR_LEN, NBR_LEN)).T
            for n in range(NEIGHBOURS)], axis=0)
        weights = [softmax(asked[u, g] * scale, 0) for g in range(GROUPS)]
        outs = [dot_first(w, panel(g, u)).astype(jnp.bfloat16) for g, w in enumerate(weights)]
        for g, out in enumerate(outs):
            for h in range(group_heads):
                lo = h * HEAD_DIM
                out_ref[u, :, pl.ds(g * width + lo, HEAD_DIM)] = out[h * SEG_LEN:(h + 1) * SEG_LEN, lo:lo + HEAD_DIM]
        return carry

    lax.fori_loop(1, seg_dev, decode_step, 0)
    for copy in behind_stats:
        copy.wait_recv()
    for copy in prior:
        copy.wait_recv()
    total3 = behind2[0]
    for k in range(1, heads_axis):
        total3 = total3 + behind2[k]
    total3 = lax.rsqrt(total3 / full_width + epsilon) * softmax_scale
    key_scale[pl.ds(0, NEIGHBOURS), :] = total3[per_device - NEIGHBOURS:]

    @pl.when(me == 0)
    def _():
        enc[:, pl.ds(0, NEIGHBOURS)] = jnp.zeros((GROUPS, NEIGHBOURS, NBR_LEN, width), jnp.bfloat16)

    for g in range(GROUPS):
        ask(g, 0)
    decode_step(0, 0)
    for copy in [handed] + list(sent.values()) + prior + first_stats + second_stats + behind_stats:
        copy.wait_send()


def fused_body(
    neighbour_query,
    neighbour_key,
    neighbour_value,
    segment_key,
    segment_value,
    decoder_query,
    sources,
):
    columns = neighbour_query.shape[1]
    heads_axis = lax.axis_size("head")
    span = lax.axis_size("span")
    per_device = SEG_DEV * NEIGHBOURS
    width = columns // GROUPS
    bf16, f32 = jnp.bfloat16, jnp.float32
    neighbour_shape = (per_device, NBR_LEN, columns)
    segment_shape = (SEG_DEV, SEG_LEN, columns)
    chunks = 2 * GROUPS
    any_space = pl.BlockSpec(memory_space=pltpu.HBM)
    dma = pltpu.SemaphoreType.DMA
    out = pl.pallas_call(
        functools.partial(kernel, heads_axis, columns * heads_axis),
        out_shape=jax.ShapeDtypeStruct(segment_shape, bf16),
        in_specs=[pl.BlockSpec(memory_space=pltpu.SMEM)] + [any_space] * 6,
        out_specs=pl.BlockSpec(memory_space=pltpu.VMEM),
        scratch_shapes=[pltpu.VMEM(neighbour_shape, bf16)] * 3
        + [pltpu.VMEM(segment_shape, bf16)]
        + [pltpu.VMEM((span * SEG_DEV, SEG_LEN, width), bf16)] * chunks
        + [
            pltpu.VMEM((GROUPS, per_device, NBR_LEN, width), bf16),
            pltpu.VMEM((GROUPS, per_device, width // HEAD_DIM * SEG_LEN, NBR_LEN), bf16),
            pltpu.VMEM((SEG_DEV, GROUPS, NEIGHBOURS * NBR_LEN, width // HEAD_DIM * SEG_LEN), f32),
            pltpu.VMEM((GROUPS, per_device + NEIGHBOURS, NBR_LEN, width), bf16),
            pltpu.VMEM((per_device, NBR_LEN, HEAD_DIM), f32),
            pltpu.VMEM((per_device, NBR_LEN), f32),
            pltpu.VMEM((per_device + NEIGHBOURS, NBR_LEN), f32),
            pltpu.VMEM((per_device, NBR_LEN), f32),
            pltpu.VMEM((per_device, NBR_LEN), f32),
            pltpu.VMEM((heads_axis - 1, per_device, NBR_LEN), f32),
            pltpu.VMEM((heads_axis - 1, per_device, NBR_LEN), f32),
            pltpu.VMEM((heads_axis, per_device, NBR_LEN), f32),
            dma((3, per_device)),
            dma,
            dma((chunks,)),
            dma((9, chunks)),
            dma((9, chunks)),
            dma((3, heads_axis)),
            dma((3, heads_axis)),
            dma((GROUPS,)),
            dma((GROUPS,)),
        ],
        compiler_params=pltpu.CompilerParams(
            collective_id=0, has_side_effects=True, vmem_limit_bytes=53 * 1024 * 1024),
    )(
        sources.T,
        neighbour_query.reshape(neighbour_shape),
        neighbour_key.reshape(neighbour_shape),
        neighbour_value.reshape(neighbour_shape),
        segment_key.reshape(segment_shape),
        segment_value.reshape(segment_shape),
        decoder_query.reshape(segment_shape),
    )
    return out.reshape(SEG_DEV * SEG_LEN, columns)


def solution(mesh):
    placed = (
        P("span", "head"),
        P("span", "head"),
        P("span", "head"),
        P("span", "head"),
        P("span", "head"),
        P("span", "head"),
        P("span", None),
    )
    cube = mesh.shape["span"] == 2 * 2 * 2
    return jax.shard_map(
        fused_body if cube else body, mesh=mesh, in_specs=placed, out_specs=P("span", "head"), check_vma=False
    )
```

```python
import functools
import math

import jax
import jax.numpy as jnp
from jax import lax
from jax.experimental import pallas as pl
from jax.experimental.pallas import tpu as pltpu
from jax.sharding import PartitionSpec as P

HEAD_DIM = 128
SEG_LEN = 64
NBR_LEN = 128
NEIGHBOURS = 2
SEG_DEV = 4


epsilon = 1e-06


def from_behind(x, axis, by):
    count = lax.axis_size(axis)
    pairs = [(i, i + by) for i in range(count) if 0 <= i + by < count]
    return lax.ppermute(x, axis, pairs)


def attend(query_rows, key_rows, value_rows):
    groups, length, columns = query_rows.shape
    head_count = columns // HEAD_DIM
    query_heads = query_rows.reshape(groups, length, head_count, HEAD_DIM)
    key_heads = key_rows.reshape(groups, key_rows.shape[1], head_count, HEAD_DIM)
    value_heads = value_rows.reshape(groups, value_rows.shape[1], head_count, HEAD_DIM)
    logit_scores = jnp.einsum(
        "bqhd,bkhd->bhqk", query_heads, key_heads, preferred_element_type=jnp.float32
    ) * HEAD_DIM ** (-0.5)
    logit_scores = logit_scores - jnp.max(logit_scores, axis=-1, keepdims=True)
    weights = jnp.exp(logit_scores)
    weights = (weights / jnp.sum(weights, axis=-1, keepdims=True)).astype(jnp.bfloat16)
    output = jnp.einsum("bhqk,bkhd->bqhd", weights, value_heads, preferred_element_type=jnp.float32)
    return output.reshape(groups, length, columns)


def squares(rows):
    wide = rows.astype(jnp.float32)
    return jnp.sum(wide * wide, axis=-1)


def normalize(rows, totals, full_width):
    scale = lax.rsqrt(totals / full_width + epsilon)
    return (rows.astype(jnp.float32) * scale[:, None]).astype(jnp.bfloat16)


def body(
    neighbour_query,
    neighbour_key,
    neighbour_value,
    segment_key,
    segment_value,
    decoder_query,
    sources,
):
    columns = neighbour_query.shape[1]
    full_width = columns * lax.axis_size("head")
    devices = lax.axis_size("span")
    per_device = SEG_DEV * NEIGHBOURS
    capacity = max(2, 2 * per_device // devices)
    panel_rows = NEIGHBOURS * NBR_LEN
    self_out = attend(
        neighbour_query.reshape(per_device, NBR_LEN, columns),
        neighbour_key.reshape(per_device, NBR_LEN, columns),
        neighbour_value.reshape(per_device, NBR_LEN, columns),
    ).astype(jnp.bfloat16)
    flat_self = self_out.reshape(per_device * NBR_LEN, columns)
    totals = lax.psum(squares(flat_self), "head")
    cross_query = normalize(flat_self, totals, full_width).reshape(per_device, NBR_LEN, columns)
    listed = sources.reshape(per_device)
    owners = listed // SEG_DEV
    within = listed % SEG_DEV
    position = jnp.arange(per_device)
    earlier = (owners[:, None] == owners[None, :]) & (position[:, None] > position[None, :])
    ranked = jnp.sum(earlier.astype(jnp.int32), axis=1)
    slots = owners * capacity + ranked
    picked = (slots[:, None] == jnp.arange(devices * capacity)[None, :]).astype(jnp.int32)
    request = jnp.sum(picked * (within + 1)[:, None], axis=0).reshape(devices, capacity)
    asked = lax.all_to_all(request, "span", split_axis=0, concat_axis=0, tiled=True)
    wanted = jnp.maximum(asked - 1, 0).reshape(devices * capacity)
    own_keys = segment_key.reshape(SEG_DEV, SEG_LEN, columns)[wanted]
    own_values = segment_value.reshape(SEG_DEV, SEG_LEN, columns)[wanted]
    got_keys, got_values = (
        lax.all_to_all(
            own_keys.reshape(devices, capacity, SEG_LEN, columns),
            "span",
            split_axis=0,
            concat_axis=0,
            tiled=True,
        ),
        lax.all_to_all(
            own_values.reshape(devices, capacity, SEG_LEN, columns),
            "span",
            split_axis=0,
            concat_axis=0,
            tiled=True,
        ),
    )
    source_keys = got_keys.reshape(devices * capacity, SEG_LEN, columns)[slots]
    source_values = got_values.reshape(devices * capacity, SEG_LEN, columns)[slots]
    crossed = attend(cross_query, source_keys, source_values).astype(jnp.bfloat16)
    encoded = (self_out.astype(jnp.float32) + crossed.astype(jnp.float32)).astype(jnp.bfloat16)
    encoded = encoded.reshape(per_device * NBR_LEN, columns)
    key_totals = lax.psum(squares(encoded), "head")
    keys_all = normalize(encoded, key_totals, full_width)
    before_keys, before_values = from_behind(
        (keys_all[-panel_rows:], encoded[-panel_rows:]), "span", 1
    )
    used_keys = jnp.concatenate([before_keys, keys_all[:-panel_rows]], axis=0)
    used_values = jnp.concatenate([before_values, encoded[:-panel_rows]], axis=0)
    blended = attend(
        decoder_query.reshape(SEG_DEV, SEG_LEN, columns),
        used_keys.reshape(SEG_DEV, panel_rows, columns),
        used_values.reshape(SEG_DEV, panel_rows, columns),
    ).astype(jnp.bfloat16)
    return blended.reshape(SEG_DEV * SEG_LEN, columns)


MESH = pl.DeviceIdType.MESH
GROUPS = 4


def dot_t(a, b):
    return lax.dot_general(a, b, (((1,), (1,)), ((), ())), preferred_element_type=jnp.float32)


def dot_first(a, b):
    return lax.dot_general(a, b, (((0,), (0,)), ((), ())), preferred_element_type=jnp.float32)


def apart(rows):
    count = rows.shape[1] // HEAD_DIM
    zero = jnp.zeros((rows.shape[0], HEAD_DIM), rows.dtype)
    lines = []
    for h in range(count):
        own = rows[:, h * HEAD_DIM:(h + 1) * HEAD_DIM]
        lines.append(jnp.concatenate([own if k == h else zero for k in range(count)], axis=1))
    return jnp.concatenate(lines, axis=0)


def softmax(scores, axis):
    weights = jnp.exp2(scores - jnp.max(scores, axis=axis, keepdims=True))
    inverse = 1.0 / jnp.sum(weights, axis=axis, keepdims=True)
    return (weights * inverse).astype(jnp.bfloat16)


def kernel(
    heads_axis, full_width,
    src_ref, nq_hbm, nk_hbm, nv_hbm, sk_hbm, sv_hbm, dq_hbm, out_ref,
    nq, nk, nv, dq, *rest,
):
    kbufs, vbufs = rest[:GROUPS], rest[GROUPS:2 * GROUPS]
    (own_out, mixing, asked, enc, squares_acc, row_scale, key_scale,
     stat1, stat2, peer1, peer2, behind2,
     in_sem, dq_sem, local_sem, send_sem, recv_sem,
     stat_send, stat_recv, prior_send, prior_recv) = rest[2 * GROUPS:]
    per_device = nq.shape[0]
    seg_dev = dq.shape[0]
    columns = nq.shape[2]
    width = columns // GROUPS
    group_heads = width // HEAD_DIM
    span = lax.axis_size("span")
    me = lax.axis_index("span")
    lane = lax.axis_index("head")
    core, across, along = me ^ 1, me ^ 2, me ^ 4
    after = lax.rem(me + 1, span)
    before = lax.rem(me + span - 1, span)
    softmax_scale = HEAD_DIM ** (-0.5) / math.log(2.0)

    barrier = pltpu.get_barrier_semaphore()
    greeted = 0
    for target in (core, across, along):
        pl.semaphore_signal(barrier, inc=1, device_id={"span": target, "head": lane}, device_id_type=MESH)
        greeted += 1
    for k in range(1, heads_axis):
        other = lax.rem(lane + k, heads_axis)
        pl.semaphore_signal(barrier, inc=1, device_id={"span": me, "head": other}, device_id_type=MESH)
        greeted += 1
    for k in range(heads_axis):
        other = lax.rem(lane + k, heads_axis)
        for target in (after, before):
            pl.semaphore_signal(barrier, inc=1, device_id={"span": target, "head": other}, device_id_type=MESH)
            greeted += 1
    pl.semaphore_wait(barrier, greeted)

    chunks = 2 * GROUPS

    def buffer(j):
        return (kbufs + vbufs)[j]

    def source(j):
        hbm = (sk_hbm, sv_hbm)[j // GROUPS]
        return hbm.at[:, :, pl.ds((j % GROUPS) * width, width)]

    def block(j, owner):
        return buffer(j).at[pl.ds(owner * seg_dev, seg_dev)]

    def half(j, owner, part):
        rows = seg_dev // 2
        return buffer(j).at[pl.ds(owner * seg_dev + part * rows, rows)]

    sent = {}

    def push(kind, j, src, dst, target):
        copy = pltpu.make_async_remote_copy(
            src_ref=src, dst_ref=dst, send_sem=send_sem.at[kind, j], recv_sem=recv_sem.at[kind, j],
            device_id={"span": target, "head": lane}, device_id_type=MESH)
        copy.start()
        sent[kind, j] = copy

    def direct(j):
        push(0, j, source(j), block(j, me), across)
        push(1, j, source(j), block(j, me), along)

    local = []
    for j in range(chunks):
        direct(j)

    for i in range(per_device):
        for a, (hbm, vm) in enumerate(((nq_hbm, nq), (nk_hbm, nk), (nv_hbm, nv))):
            pltpu.make_async_copy(hbm.at[i], vm.at[i], in_sem.at[a, i]).start()
    dq_copy = pltpu.make_async_copy(dq_hbm, dq, dq_sem)
    dq_copy.start()

    for j in range(chunks):
        push(4, j, source(j), block(j, me), core)
        copy = pltpu.make_async_copy(source(j), block(j, me), local_sem.at[j])
        copy.start()
        local.append(copy)

    def forward(j):
        for part in range(2):
            sent[2 + part, j].wait_recv()
            push(7 + part, j, half(j, me ^ 6, part), half(j, me ^ 6, part), core)

    def step(j):
        sent[1, j].wait_recv()
        push(2, j, half(j, along, 0), half(j, along, 0), across)
        sent[0, j].wait_recv()
        push(3, j, half(j, across, 1), half(j, across, 1), along)
        push(5, j, block(j, across), block(j, across), core)
        push(6, j, block(j, along), block(j, along), core)

    def arrived(j):
        local[j].wait()
        for kind in (4, 5, 6, 7, 8):
            sent[kind, j].wait_recv()

    def self_step(i, carry):
        for a, (hbm, vm) in enumerate(((nq_hbm, nq), (nk_hbm, nk), (nv_hbm, nv))):
            pltpu.make_async_copy(hbm.at[i], vm.at[i], in_sem.at[a, i]).wait()
        total = jnp.zeros((NBR_LEN, HEAD_DIM), jnp.float32)
        for base in range(0, columns // HEAD_DIM, 8):
            together = range(base, base + 8)
            cols = [pl.ds(h * HEAD_DIM, HEAD_DIM) for h in together]
            scores = [dot_t(nk[i, :, c], nq[i, :, c]) * softmax_scale for c in cols]
            weights = [softmax(x, 0) for x in scores]
            outs = [dot_first(w, nv[i, :, c]).astype(jnp.bfloat16) for w, c in zip(weights, cols)]
            for h, o in zip(together, outs):
                own_out[h // group_heads, i, :, pl.ds((h % group_heads) * HEAD_DIM, HEAD_DIM)] = o
                wide = o.astype(jnp.float32)
                total = total + wide * wide
        stat1[pl.ds(i, 1), :] = jnp.sum(total.T, axis=0, keepdims=True)
        return carry

    def exchange(kind, stat, peer):
        out = []
        for k in range(1, heads_axis):
            other = lax.rem(lane + k, heads_axis)
            copy = pltpu.make_async_remote_copy(
                src_ref=stat, dst_ref=peer.at[k - 1],
                send_sem=stat_send.at[kind, k - 1], recv_sem=stat_recv.at[kind, k - 1],
                device_id={"span": me, "head": other}, device_id_type=MESH)
            copy.start()
            out.append(copy)
        return out

    def weigh(g):
        arrived(g)

        def some(t, carry):
            rows = [4 * t + b for b in range(4)]
            keys = [apart(kbufs[g][src_ref[i % NEIGHBOURS, i // NEIGHBOURS]]) for i in rows]
            scores = [dot_t(k, own_out[g, i]) * row_scale[pl.ds(i, 1), :] for k, i in zip(keys, rows)]
            weights = [softmax(x.reshape(group_heads, SEG_LEN, NBR_LEN), 1) for x in scores]
            for i, w in zip(rows, weights):
                mixing[g, i] = w.reshape(group_heads * SEG_LEN, NBR_LEN)
            return carry

        lax.fori_loop(0, per_device // 4, some, 0)

    def cross_rows(g, rows):
        values = [apart(vbufs[g][src_ref[i % NEIGHBOURS, i // NEIGHBOURS]]) for i in rows]
        crossed = [dot_first(mixing[g, i], v).astype(jnp.bfloat16) for i, v in zip(rows, values)]
        for i, x in zip(rows, crossed):
            both = (own_out[g, i].astype(jnp.float32) + x.astype(jnp.float32)).astype(jnp.bfloat16)
            enc[g, NEIGHBOURS + i] = both
            wide = both.astype(jnp.float32)
            wide = wide * wide
            total = wide[:, :HEAD_DIM]
            for h in range(1, group_heads):
                total = total + wide[:, h * HEAD_DIM:(h + 1) * HEAD_DIM]
            if g > 0:
                total = total + squares_acc[i]
            if g < GROUPS - 1:
                squares_acc[i] = total
            else:
                stat2[pl.ds(i, 1), :] = jnp.sum(total.T, axis=0, keepdims=True)

    prior = []

    def panel(g, u):
        return enc[g, pl.ds(NEIGHBOURS * u, NEIGHBOURS)].reshape(NEIGHBOURS * NBR_LEN, width)

    def ask(g, u):
        asked[u, g] = dot_t(panel(g, u), apart(dq[u, :, pl.ds(g * width, width)]))

    def cross(g):
        arrived(GROUPS + g)
        cross_rows(g, list(range(per_device - NEIGHBOURS, per_device)))
        copy = pltpu.make_async_remote_copy(
            src_ref=enc.at[g, pl.ds(per_device, NEIGHBOURS)], dst_ref=enc.at[g, pl.ds(0, NEIGHBOURS)],
            send_sem=prior_send.at[g], recv_sem=prior_recv.at[g],
            device_id={"span": after, "head": lane}, device_id_type=MESH)
        copy.start()
        prior.append(copy)

        def rest_step(t, carry):
            cross_rows(g, [3 * t + b for b in range(3)])
            return carry

        lax.fori_loop(0, (per_device - NEIGHBOURS) // 3, rest_step, 0)

    quarter = per_device // 4
    for j in range(4):
        lax.fori_loop(j * quarter, (j + 1) * quarter, self_step, 0)
        if j > 0:
            step(2 * j - 2)
            step(2 * j - 1)
    first_stats = exchange(0, stat1, peer1)
    step(6)
    for copy in first_stats:
        copy.wait_recv()
    total1 = stat1[...]
    for k in range(heads_axis - 1):
        total1 = total1 + peer1[k]
    row_scale[...] = lax.rsqrt(total1 / full_width + epsilon) * softmax_scale
    step(7)
    forward(0)
    for g in range(GROUPS):
        forward(g + 1)
        weigh(g)
    dq_copy.wait()
    for g in range(GROUPS):
        if g + 1 < GROUPS:
            forward(GROUPS + 1 + g)
        cross(g)
        if g + 1 < GROUPS:
            for u in range(1, seg_dev):
                ask(g, u)

    second_stats = exchange(1, stat2, peer2)
    behind_stats = []
    for k in range(heads_axis):
        other = lax.rem(lane + k, heads_axis)
        copy = pltpu.make_async_remote_copy(
            src_ref=stat2, dst_ref=behind2.at[k],
            send_sem=stat_send.at[2, k], recv_sem=stat_recv.at[2, k],
            device_id={"span": after, "head": other}, device_id_type=MESH)
        copy.start()
        behind_stats.append(copy)
    for u in range(1, seg_dev):
        ask(GROUPS - 1, u)
    for copy in second_stats:
        copy.wait_recv()
    total2 = stat2[...]
    for k in range(heads_axis - 1):
        total2 = total2 + peer2[k]
    key_scale[pl.ds(NEIGHBOURS, per_device), :] = lax.rsqrt(total2 / full_width + epsilon) * softmax_scale

    def decode_step(u, carry):
        scale = jnp.concatenate([
            jnp.broadcast_to(key_scale[pl.ds(NEIGHBOURS * u + n, 1), :], (NBR_LEN, NBR_LEN)).T
            for n in range(NEIGHBOURS)], axis=0)
        weights = [softmax(asked[u, g] * scale, 0) for g in range(GROUPS)]
        outs = [dot_first(w, panel(g, u)).astype(jnp.bfloat16) for g, w in enumerate(weights)]
        for g, out in enumerate(outs):
            for h in range(group_heads):
                lo = h * HEAD_DIM
                out_ref[u, :, pl.ds(g * width + lo, HEAD_DIM)] = out[h * SEG_LEN:(h + 1) * SEG_LEN, lo:lo + HEAD_DIM]
        return carry

    lax.fori_loop(1, seg_dev, decode_step, 0)
    for copy in behind_stats:
        copy.wait_recv()
    for copy in prior:
        copy.wait_recv()
    total3 = behind2[0]
    for k in range(1, heads_axis):
        total3 = total3 + behind2[k]
    total3 = lax.rsqrt(total3 / full_width + epsilon) * softmax_scale
    key_scale[pl.ds(0, NEIGHBOURS), :] = total3[per_device - NEIGHBOURS:]

    @pl.when(me == 0)
    def _():
        enc[:, pl.ds(0, NEIGHBOURS)] = jnp.zeros((GROUPS, NEIGHBOURS, NBR_LEN, width), jnp.bfloat16)

    for g in range(GROUPS):
        ask(g, 0)
    decode_step(0, 0)
    for copy in list(sent.values()) + prior + first_stats + second_stats + behind_stats:
        copy.wait_send()


def fused_body(
    neighbour_query,
    neighbour_key,
    neighbour_value,
    segment_key,
    segment_value,
    decoder_query,
    sources,
):
    columns = neighbour_query.shape[1]
    heads_axis = lax.axis_size("head")
    span = lax.axis_size("span")
    per_device = SEG_DEV * NEIGHBOURS
    width = columns // GROUPS
    bf16, f32 = jnp.bfloat16, jnp.float32
    neighbour_shape = (per_device, NBR_LEN, columns)
    segment_shape = (SEG_DEV, SEG_LEN, columns)
    chunks = 2 * GROUPS
    any_space = pl.BlockSpec(memory_space=pltpu.HBM)
    dma = pltpu.SemaphoreType.DMA
    out = pl.pallas_call(
        functools.partial(kernel, heads_axis, columns * heads_axis),
        out_shape=jax.ShapeDtypeStruct(segment_shape, bf16),
        in_specs=[pl.BlockSpec(memory_space=pltpu.SMEM)] + [any_space] * 6,
        out_specs=pl.BlockSpec(memory_space=pltpu.VMEM),
        scratch_shapes=[pltpu.VMEM(neighbour_shape, bf16)] * 3
        + [pltpu.VMEM(segment_shape, bf16)]
        + [pltpu.VMEM((span * SEG_DEV, SEG_LEN, width), bf16)] * chunks
        + [
            pltpu.VMEM((GROUPS, per_device, NBR_LEN, width), bf16),
            pltpu.VMEM((GROUPS, per_device, width // HEAD_DIM * SEG_LEN, NBR_LEN), bf16),
            pltpu.VMEM((SEG_DEV, GROUPS, NEIGHBOURS * NBR_LEN, width // HEAD_DIM * SEG_LEN), f32),
            pltpu.VMEM((GROUPS, per_device + NEIGHBOURS, NBR_LEN, width), bf16),
            pltpu.VMEM((per_device, NBR_LEN, HEAD_DIM), f32),
            pltpu.VMEM((per_device, NBR_LEN), f32),
            pltpu.VMEM((per_device + NEIGHBOURS, NBR_LEN), f32),
            pltpu.VMEM((per_device, NBR_LEN), f32),
            pltpu.VMEM((per_device, NBR_LEN), f32),
            pltpu.VMEM((heads_axis - 1, per_device, NBR_LEN), f32),
            pltpu.VMEM((heads_axis - 1, per_device, NBR_LEN), f32),
            pltpu.VMEM((heads_axis, per_device, NBR_LEN), f32),
            dma((3, per_device)),
            dma,
            dma((chunks,)),
            dma((9, chunks)),
            dma((9, chunks)),
            dma((3, heads_axis)),
            dma((3, heads_axis)),
            dma((GROUPS,)),
            dma((GROUPS,)),
        ],
        compiler_params=pltpu.CompilerParams(
            collective_id=0, has_side_effects=True, vmem_limit_bytes=53 * 1024 * 1024),
    )(
        sources.T,
        neighbour_query.reshape(neighbour_shape),
        neighbour_key.reshape(neighbour_shape),
        neighbour_value.reshape(neighbour_shape),
        segment_key.reshape(segment_shape),
        segment_value.reshape(segment_shape),
        decoder_query.reshape(segment_shape),
    )
    return out.reshape(SEG_DEV * SEG_LEN, columns)


def solution(mesh):
    placed = (
        P("span", "head"),
        P("span", "head"),
        P("span", "head"),
        P("span", "head"),
        P("span", "head"),
        P("span", "head"),
        P("span", None),
    )
    cube = mesh.shape["span"] == 2 * 2 * 2
    return jax.shard_map(
        fused_body if cube else body, mesh=mesh, in_specs=placed, out_specs=P("span", "head"), check_vma=False
    )
```
